128 devices in a mesh: grp: 4 (over z_lo, core), pw: 32 (over y, z_hi, x).
Axes of the slice: x: 4, y: 4, z: 4 (z_hi: 2, z_lo: 2; z = z_hi * 2 + z_lo), core: 2. Of those that a mesh axis runs over, the one named last changes fastest.
Arguments:
- row_orbitals: bfloat16 [16, 131072], P('grp', 'pw'), may hold values from -6 to 6
- orbitals: bfloat16 [512, 131072], P(None, 'pw'), may hold values from -6 to 6
- fitting: bfloat16 [131072, 1024], P('pw'), may hold values from -0.015625 to 0.015625
- partner_vertex: bfloat16 [16, 512, 1024], P('grp', 'pw'), may hold values from -6 to 6
- amplitudes: bfloat16 [256, 512, 512], P(None, 'pw'), may hold values from -0.00036621094 to 0.00036621094
Outputs:
- ladder: float32 [256, 16, 16], P('pw', 'grp')
The draws below stay inside these ranges and needn't reach their ends.
All inputs are finite; a program needn't handle non-finite values.
Results may differ from the reference program's by a relative error of at most 0.005.
Values may be sent and summed in bfloat16 or wider, within the bound.
A program may use at most 128 MiB of HBM per device.

```python
import jax
import jax.numpy as jnp
from jax import lax

NV = 512
NAUX = 1024
GRID = 131072
ROWS = 16
PARTNERS = 16
NPAIR = 256


def levels(own_key, shape, split, smallest, high):
    factor_of, own = 1.0, jax.random.fold_in(own_key, 6)
    for dim, parts in split:
        steps = jnp.exp(jax.random.uniform(jax.random.fold_in(own, dim), (parts,), jnp.float32, smallest / len(split), high / len(split)))
        factor_of = factor_of * jnp.repeat(steps, shape[dim] // parts).reshape([-1 if axis == dim else 1 for axis in range(len(shape))])
    return factor_of


def noise(rng, extent, deviation, most, shards=(), kind=jnp.bfloat16):
    drawn = jax.random.normal(rng, extent, jnp.float32) * deviation
    if len(shards) > 0:
        drawn = levels(rng, extent, shards, -0.22, 0.18) * drawn
    return jnp.clip(drawn, min=-most, max=most).astype(kind)


def setup_inputs(seed: int = 0) -> dict:
    splits = jax.random.split(jax.random.key(seed), 6)
    return {
        "row_orbitals": noise(splits[0], (ROWS, GRID), 1.0, 6.0, ((0, 4), (1, 32))),
        "orbitals": noise(splits[1], (NV, GRID), 1.0, 6.0, ((1, 32),)),
        "fitting": noise(splits[2], (GRID, NAUX), GRID ** -0.5, 0.015625, ((0, 32),)),
        "partner_vertex": noise(splits[3], (PARTNERS, NV, NAUX), 1.0, 6.0, ((0, 4), (1, 32))),
        "amplitudes": noise(splits[4], (NPAIR, NV, NV), (NV * NV * NAUX) ** -0.5, 0.00036621094, ((1, 32),)),
    }


def reference(row_orbitals, orbitals, fitting, partner_vertex, amplitudes):
    orbit32 = orbitals.astype(jnp.float32)

    def one_row(row):
        pair = (row.astype(jnp.float32)[None, :] * orbit32).astype(jnp.bfloat16)
        return jnp.dot(pair, fitting, preferred_element_type=jnp.float32).astype(jnp.bfloat16)

    vertex = lax.map(one_row, row_orbitals)
    flat_partner = partner_vertex.reshape(PARTNERS * NV, NAUX)
    amp32 = amplitudes.astype(jnp.float32)

    def ladder_row(vrow):
        rungs = jnp.dot(vrow, flat_partner.T, preferred_element_type=jnp.float32).astype(jnp.bfloat16)
        rungs = rungs.reshape(NV, PARTNERS, NV).astype(jnp.float32)
        return jnp.einsum('cbd,icd->ib', rungs, amp32)

    result = lax.map(ladder_row, vertex)
    return jnp.transpose(result, (1, 0, 2))
```

```python
import jax
import jax.numpy as jnp
from jax import lax
from jax.experimental import pallas as pl
from jax.experimental.pallas import tpu as pltpu
from jax.sharding import PartitionSpec as P

MESH = pl.DeviceIdType.MESH
BF = jnp.bfloat16
F32 = jnp.float32
NT = 256


def kernel(
    rows_h, orb_h, fit_h, pv_h, amp_h, out_ref,
    rows_v, rowsb, orb, fit, pair, part, r1, r2, r3, t3, s1, u1, u2, u3, v3, s2, s2b, zr,
    vall, vperm, pvall, amp, ampt, rg, lp, lr, fr, perm,
    ld, ag_s, ag_r, rs_s, rs_r, st_s, st_r, z_s, z_r, gp_s, gp_r, fn_s, fn_r, fg_s, fg_r,
):
    g = lax.axis_index("grp")
    w = lax.axis_index("pw")
    y, zh, x = w // 8, lax.rem(w // 4, 2), lax.rem(w, 4)
    ng = rows_v.shape[1]
    na = fit.shape[1]
    g_core, g_chip = g + 1 - 2 * lax.rem(g, 2), lax.rem(g + 2, 4)

    def dev(yy, zz, xx):
        return (g, yy * 8 + zz * 4 + xx)

    def up(v, by=1):
        return lax.rem(v + by, 4)

    def send(src, dst, ss, rs, to):
        return pltpu.make_async_remote_copy(
            src_ref=src, dst_ref=dst, send_sem=ss, recv_sem=rs, device_id=to, device_id_type=MESH
        )

    barrier = pltpu.get_barrier_semaphore()

    @pl.loop(1, 32)
    def _(j):
        pl.semaphore_signal(barrier, inc=1, device_id=(g, lax.rem(w + j, 32)), device_id_type=MESH)

    @pl.loop(1, 4)
    def _(j):
        pl.semaphore_signal(barrier, inc=1, device_id=(lax.rem(g + j, 4), w), device_id_type=MESH)

    l_rows = pltpu.make_async_copy(rows_h, rows_v, ld.at[0])
    l_orb = pltpu.make_async_copy(orb_h, orb, ld.at[1])
    l_fit = pltpu.make_async_copy(fit_h, fit, ld.at[2])
    l_amp = pltpu.make_async_copy(amp_h, amp, ld.at[3])
    l_pv = pltpu.make_async_copy(pv_h, pvall.at[:, y, zh, x], ld.at[4])
    for c in (l_pv, l_rows, l_orb, l_fit, l_amp):
        c.start()

    ii = lax.broadcasted_iota(jnp.int32, (256, 256), 0)
    jj = lax.broadcasted_iota(jnp.int32, (256, 256), 1)
    perm[...] = jnp.where(
        jj == lax.rem(ii, 16) * 16 + ii // 16, jnp.float32(1), jnp.float32(0)
    ).astype(BF)

    pl.semaphore_wait(barrier, 34)

    ring = {0: (dev(y, zh, up(x)), dev(y, zh, up(x, 3))), 1: (dev(up(y), zh, x), dev(up(y, 3), zh, x))}

    def ag(i, ref, to):
        return send(ref, ref, ag_s.at[i], ag_r.at[i], to)

    zs = (zh, 1 - zh)
    ag_z = send(pv_h, pvall.at[:, y, zh, x], ag_s.at[0], ag_r.at[0], dev(y, 1 - zh, x))
    ag1, ag1f, ag2, ag2f = {}, {}, {}, {}
    n = 1
    for f in (0, 1):
        for h in (0, 1):
            for side in (0, 1):
                to = ring[f][side]
                src = pv_h.at[2 * f : 2 * f + 2] if h == 0 else pvall.at[2 * f : 2 * f + 2, y, zs[h], x]
                ag1[f, h, side] = send(
                    src, pvall.at[2 * f : 2 * f + 2, y, zs[h], x], ag_s.at[n], ag_r.at[n], to
                )
                back = 3 if side == 0 else 1
                b = 2 * f + side
                ref = pvall.at[b, y, zs[h], up(x, back)] if f == 0 else pvall.at[b, up(y, back), zs[h], x]
                ag1f[f, h, side] = ag(n + 1, ref, to)
                n += 2
    for f in (0, 1):
        for side in (0, 1):
            to = ring[1 - f][side]
            ref = pvall.at[0:2, y] if f == 0 else pvall.at[2:4, :, :, x]
            ag2[f, side] = ag(n, ref, to)
            back = 3 if side == 0 else 1
            b = 2 * f + side
            ref = pvall.at[b, up(y, back)] if f == 0 else pvall.at[b, :, :, up(x, back)]
            ag2f[f, side] = ag(n + 1, ref, to)
            n += 2

    for f in (0, 1):
        for side in (0, 1):
            ag1[f, 0, side].start()
    ag_z.start()

    def geo(s):
        f, k = lax.rem(s, 2), s // 2
        q = jnp.where(f == 0, x, y)
        right = dev(up(y, f), zh, up(x, 1 - f))
        left = dev(up(y, 4 - f), zh, up(x, 3 + f))
        return f, k, q, right, left

    def rs(s, m):
        _, _, q, right, left = geo(s)
        src, dst, to = {
            0: (part.at[s, up(q, 2), 0:32], r1.at[s, 0], right),
            1: (part.at[s, up(q, 2), 32:64], r1.at[s, 1], left),
            2: (part.at[s, up(q, 1), 32:64], r2.at[s, 0], right),
            3: (part.at[s, up(q, 3), 0:32], r2.at[s, 1], left),
            4: (t3.at[s, 0], r3.at[s, 0], right),
            5: (t3.at[s, 1], r3.at[s, 1], left),
        }[m]
        return send(src, dst, rs_s.at[s, m], rs_r.at[s, m], to)

    def st(f, m):
        right = dev(up(y, 1 - f), zh, up(x, f))
        left = dev(up(y, 3 + f), zh, up(x, 4 - f))
        src, dst, to = {
            0: (s1.at[f, 0, 0:32], u1.at[f, 0], right),
            1: (s1.at[f, 0, 32:64], u1.at[f, 1], left),
            2: (s1.at[f, 1, 32:64], u2.at[f, 0], right),
            3: (s1.at[f, 2, 0:32], u2.at[f, 1], left),
            4: (v3.at[f, 0], u3.at[f, 0], right),
            5: (v3.at[f, 1], u3.at[f, 1], left),
        }[m]
        return send(src, dst, st_s.at[f, m], st_r.at[f, m], to)

    def middle(s):
        _, _, q, _, _ = geo(s)
        rs(s, 0).wait_recv()
        t3[s, 0] = (part[s, up(q, 1), 0:32].astype(F32) + r1[s, 0].astype(F32)).astype(BF)
        rs(s, 4).start()
        rs(s, 1).wait_recv()
        t3[s, 1] = (part[s, up(q, 3), 32:64].astype(F32) + r1[s, 1].astype(F32)).astype(BF)
        rs(s, 5).start()

    def finish(s):
        f, k, q, _, _ = geo(s)
        for m in (2, 3, 4, 5):
            rs(s, m).wait_recv()
        s1[f, k, 0:32] = (
            part[s, q, 0:32].astype(F32) + r3[s, 0].astype(F32) + r2[s, 1].astype(F32)
        ).astype(BF)
        s1[f, k, 32:64] = (
            part[s, q, 32:64].astype(F32) + r2[s, 0].astype(F32) + r3[s, 1].astype(F32)
        ).astype(BF)

        @pl.when(k == 0)
        def _():
            st(f, 0).start()
            st(f, 1).start()

        @pl.when(k == 1)
        def _():
            st(f, 2).start()

        @pl.when(k == 2)
        def _():
            st(f, 3).start()

    l_rows.wait()
    for a in range(4):
        rowsb[a] = jnp.broadcast_to(rows_v[a : a + 1, :], (16, ng))
    l_orb.wait()
    l_fit.wait()

    @pl.loop(0, 8)
    def _(s):
        f, k, _, _, _ = geo(s)
        off = jnp.where(k == 0, 2, jnp.where(k == 1, 1, jnp.where(k == 2, 3, 0)))
        for j in range(4):
            c0 = (1 - f) * (128 * up(y, off) + 16 * j) + f * (128 * j + 64 + 16 * up(x, off))
            ob = orb[pl.ds(pl.multiple_of(c0, 16), 16), :]
            for a in range(4):
                pair[j * 64 + a * 16 : j * 64 + a * 16 + 16, :] = rowsb[a] * ob
        for t in range(na // NT):
            acc = jnp.dot(pair[...], fit[:, t * NT : (t + 1) * NT], preferred_element_type=F32)
            part[s, :, :, t * NT : (t + 1) * NT] = acc.astype(BF).reshape(4, 64, NT)
        for m in range(4):
            rs(s, m).start()

        @pl.when(s == 0)
        def _():
            ag_z.wait_recv()
            for ff in (0, 1):
                for side in (0, 1):
                    ag1[ff, 1, side].start()
            for ff in (0, 1):
                for side in (0, 1):
                    ag1[ff, 0, side].wait_recv()
            for ff in (0, 1):
                for side in (0, 1):
                    ag1f[ff, 0, side].start()

        @pl.when(s == 1)
        def _():
            for ff in (0, 1):
                for side in (0, 1):
                    ag1[ff, 1, side].wait_recv()
            for ff in (0, 1):
                for side in (0, 1):
                    ag1f[ff, 1, side].start()

        @pl.when(s >= 1)
        def _():
            middle(s - 1)

        @pl.when(s >= 3)
        def _():
            finish(s - 3)

    middle(7)
    finish(5)
    for f in (0, 1):
        st(f, 0).wait_recv()
        v3[f, 0] = (s1[f, 1, 0:32].astype(F32) + u1[f, 0].astype(F32)).astype(BF)
        st(f, 4).start()
        st(f, 1).wait_recv()
        v3[f, 1] = (s1[f, 2, 32:64].astype(F32) + u1[f, 1].astype(F32)).astype(BF)
        st(f, 5).start()

    for f in (0, 1):
        for h in (0, 1):
            for side in (0, 1):
                ag1f[f, h, side].wait_recv()
    l_pv.wait()
    for f in (0, 1):
        for side in (0, 1):
            ag2[f, side].start()

    for f in (0, 1):
        finish(6 + f)
        for m in (2, 3, 4, 5):
            st(f, m).wait_recv()
        lo = s1[f, 3, 0:32].astype(F32) + u3[f, 0].astype(F32) + u2[f, 1].astype(F32)
        hi = s1[f, 3, 32:64].astype(F32) + u2[f, 0].astype(F32) + u3[f, 1].astype(F32)
        s2[f, 0:32] = lo
        s2[f, 32:64] = hi
        s2b[f, 0:32] = lo.astype(BF)
        s2b[f, 32:64] = hi.astype(BF)
    zsend = send(s2b.at[1 - zh], zr, z_s, z_r, dev(y, 1 - zh, x))
    zsend.start()

    l_amp.wait()

    @pl.loop(0, 16)
    def _(i):
        i0 = pl.multiple_of(i * 16, 16)
        blk = amp[pl.ds(i0, 16)].reshape(256, 512)
        turned = jnp.dot(perm[...], blk, preferred_element_type=F32).astype(BF)
        ampt[:, pl.ds(i0, 16), :] = turned.reshape(16, 16, 512)

    zsend.wait_recv()
    vall[g] = (s2[zh] + zr[...].astype(F32)).astype(BF)
    gp_chip = send(vall.at[g], vall.at[g], gp_s.at[0], gp_r.at[0], (g_chip, w))
    gp_core = send(vall.at[g], vall.at[g], gp_s.at[1], gp_r.at[1], (g_core, w))
    gp_fwd = send(vall.at[g_chip], vall.at[g_chip], gp_s.at[2], gp_r.at[2], (g_core, w))
    gp_chip.start()
    gp_core.start()

    for f in (0, 1):
        for side in (0, 1):
            ag2[f, side].wait_recv()
    for f in (0, 1):
        for side in (0, 1):
            ag2f[f, side].start()
    gp_chip.wait_recv()
    gp_fwd.start()
    gp_core.wait_recv()
    gp_fwd.wait_recv()

    vperm[...] = jnp.dot(perm[...], vall[...].reshape(256, na), preferred_element_type=F32).astype(BF)
    for f in (0, 1):
        for side in (0, 1):
            ag2f[f, side].wait_recv()

    nt = (((1,), (1,)), ((), ()))
    for b in range(4):
        rung = lax.dot_general(vperm[...], pvall[b].reshape(512, na), nt, preferred_element_type=F32)
        rg[:, b * 16 : b * 16 + 16, :] = rung.astype(BF).reshape(16, 16, 512)
    acc = jnp.zeros((256, 64), F32)
    for c in range(16):
        acc += lax.dot_general(ampt[c], rg[c], nt, preferred_element_type=F32)
    lp[:, :, 0:64] = acc.reshape(32, 8, 64)
    lp[:, :, 64:128] = jnp.zeros((32, 8, 64), F32)

    def fn(j):
        to = lax.rem(w + j, 32)
        return send(lp.at[to], lr.at[j], fn_s.at[j], fn_r.at[j], (g, to))

    @pl.loop(1, 32)
    def _(j):
        fn(j).start()

    total = lp[w]
    for j in range(1, 32):
        fn(j).wait_recv()
    for j in range(1, 32):
        total += lr[j]
    fr[g] = total

    def fg(j):
        return send(fr.at[g], fr.at[g], fg_s.at[j], fg_r.at[j], (lax.rem(g + j, 4), w))

    for j in (1, 2, 3):
        fg(j).start()
    for j in (1, 2, 3):
        fg(j).wait_recv()
    rr = lax.broadcasted_iota(jnp.int32, (128, 64), 0)
    cc = lax.broadcasted_iota(jnp.int32, (128, 64), 1)
    res = jnp.zeros((8, 64), F32)
    for p in range(4):
        pick = (lax.rem(rr, 16) == g * 4 + cc // 16) & (p * 4 + rr // 16 == lax.rem(cc, 16))
        res += jnp.dot(
            fr[p], jnp.where(pick, jnp.float32(1), jnp.float32(0)),
            precision=lax.Precision.HIGHEST, preferred_element_type=F32,
        )
    out_ref[...] = res

    ag_z.wait_send()
    for f in (0, 1):
        for side in (0, 1):
            for h in (0, 1):
                ag1[f, h, side].wait_send()
                ag1f[f, h, side].wait_send()
            ag2[f, side].wait_send()
            ag2f[f, side].wait_send()
        for m in range(6):
            st(f, m).wait_send()

    @pl.loop(0, 8)
    def _(s):
        for m in range(6):
            rs(s, m).wait_send()

    for c in (zsend, gp_chip, gp_core, gp_fwd):
        c.wait_send()

    @pl.loop(1, 32)
    def _(j):
        fn(j).wait_send()

    for j in (1, 2, 3):
        fg(j).wait_send()


def local(row_orbitals, orbitals, fitting, partner_vertex, amplitudes):
    ng, na = fitting.shape
    dma = pltpu.SemaphoreType.DMA
    half = (32, na)
    out = pl.pallas_call(
        kernel,
        out_shape=jax.ShapeDtypeStruct((8, 64), F32),
        in_specs=[pl.BlockSpec(memory_space=pl.ANY)] * 5,
        out_specs=pl.BlockSpec(memory_space=pltpu.VMEM),
        scratch_shapes=[
            pltpu.VMEM((4, ng), BF),
            pltpu.VMEM((4, 16, ng), BF),
            pltpu.VMEM((512, ng), BF),
            pltpu.VMEM((ng, na), BF),
            pltpu.VMEM((256, ng), BF),
            pltpu.VMEM((8, 4, 64, na), BF),
            pltpu.VMEM((8, 2, *half), BF),
            pltpu.VMEM((8, 2, *half), BF),
            pltpu.VMEM((8, 2, *half), BF),
            pltpu.VMEM((8, 2, *half), BF),
            pltpu.VMEM((2, 4, 64, na), BF),
            pltpu.VMEM((2, 2, *half), BF),
            pltpu.VMEM((2, 2, *half), BF),
            pltpu.VMEM((2, 2, *half), BF),
            pltpu.VMEM((2, 2, *half), BF),
            pltpu.VMEM((2, 64, na), F32),
            pltpu.VMEM((2, 64, na), BF),
            pltpu.VMEM((64, na), BF),
            pltpu.VMEM((4, 64, na), BF),
            pltpu.VMEM((256, na), BF),
            pltpu.VMEM((4, 4, 2, 4, 16, na), BF),
            pltpu.VMEM((256, 16, 512), BF),
            pltpu.VMEM((16, 256, 512), BF),
            pltpu.VMEM((16, 64, 512), BF),
            pltpu.VMEM((32, 8, 128), F32),
            pltpu.VMEM((32, 8, 128), F32),
            pltpu.VMEM((4, 8, 128), F32),
            pltpu.VMEM((256, 256), BF),
            dma((5,)),
            dma((25,)), dma((25,)),
            dma((8, 6)), dma((8, 6)),
            dma((2, 6)), dma((2, 6)),
            dma, dma,
            dma((3,)), dma((3,)),
            dma((32,)), dma((32,)),
            dma((4,)), dma((4,)),
        ],
        compiler_params=pltpu.CompilerParams(
            collective_id=0, has_side_effects=True, vmem_limit_bytes=60 * 1024 * 1024
        ),
    )(row_orbitals, orbitals, fitting, partner_vertex, amplitudes)
    return out.reshape(8, 4, 16)


def solution(mesh):
    in_specs = (P("grp", "pw"), P(None, "pw"), P("pw", None), P("grp", "pw", None), P(None, "pw", None))
    return jax.shard_map(
        local, mesh=mesh, in_specs=in_specs, out_specs=P("pw", "grp", None), check_vma=False
    )
```

```python
import jax
import jax.numpy as jnp
from jax import lax
from jax.experimental import pallas as pl
from jax.experimental.pallas import tpu as pltpu
from jax.sharding import PartitionSpec as P

MESH = pl.DeviceIdType.MESH
BF = jnp.bfloat16
F32 = jnp.float32
NT = 256


def kernel(
    rows_h, orb_h, fit_h, pv_h, amp_h, out_ref,
    rows_v, rowsb, orb, fit, pair, part, r1, r2, r3, t3, s1, u1, u2, u3, v3, s2, s2b, zr,
    vall, vperm, pvall, amp, ah, ampb, ampt, rg, lp, lr, fr, perm,
    ld, ag_s, ag_r, rs_s, rs_r, st_s, st_r, z_s, z_r, ve_s, ve_r, am_s, am_r, fn_s, fn_r, fg_s, fg_r,
):
    g = lax.axis_index("grp")
    w = lax.axis_index("pw")
    y, zh, x = w // 8, lax.rem(w // 4, 2), lax.rem(w, 4)
    ng = rows_v.shape[1]
    na = fit.shape[1]
    core = lax.rem(g, 2)
    g_core, g_chip = g + 1 - 2 * core, lax.rem(g + 2, 4)
    w_far = w + 4 - 8 * zh

    def dev(yy, zz, xx):
        return (g, yy * 8 + zz * 4 + xx)

    def up(v, by=1):
        return lax.rem(v + by, 4)

    def send(src, dst, ss, rs, to):
        return pltpu.make_async_remote_copy(
            src_ref=src, dst_ref=dst, send_sem=ss, recv_sem=rs, device_id=to, device_id_type=MESH
        )

    barrier = pltpu.get_barrier_semaphore()

    @pl.loop(1, 32)
    def _(j):
        pl.semaphore_signal(barrier, inc=1, device_id=(g, lax.rem(w + j, 32)), device_id_type=MESH)

    @pl.loop(1, 4)
    def _(j):
        pl.semaphore_signal(barrier, inc=1, device_id=(lax.rem(g + j, 4), w), device_id_type=MESH)

    pl.semaphore_signal(barrier, inc=1, device_id=(g_chip, w_far), device_id_type=MESH)

    def piece(d, z):
        rows = pl.ds(pl.multiple_of(128 * up(y, 2 + d) + 64 * z, 64), 64)
        return pltpu.make_async_copy(orb_h.at[rows, :], orb.at[rows, :], ld.at[7 + 4 * z + d])

    def fit_tile(t):
        rows = slice(t * (ng // 4), (t + 1) * (ng // 4))
        return pltpu.make_async_copy(fit_h.at[rows], fit.at[rows], ld.at[3 + t])

    tiles = na // NT
    l_rows = pltpu.make_async_copy(rows_h, rows_v, ld.at[0])
    l_amp = pltpu.make_async_copy(amp_h, amp, ld.at[1])
    l_pv = pltpu.make_async_copy(pv_h, pvall.at[:, y, x], ld.at[2])
    for c in (l_rows, l_amp, piece(0, 0), *(fit_tile(t) for t in range(4)), l_pv):
        c.start()

    ii = lax.broadcasted_iota(jnp.int32, (256, 256), 0)
    jj = lax.broadcasted_iota(jnp.int32, (256, 256), 1)
    perm[...] = jnp.where(
        jj == lax.rem(ii, 16) * 16 + ii // 16, jnp.float32(1), jnp.float32(0)
    ).astype(BF)

    ring = {0: (dev(y, zh, up(x)), dev(y, zh, up(x, 3))), 1: (dev(up(y), zh, x), dev(up(y, 3), zh, x))}
    ag1, ag1f, ag2, ag2f = {}, {}, {}, {}
    n = 0

    def ag(into, key, src, ref, to):
        nonlocal n
        into[key] = send(src, ref, ag_s.at[n], ag_r.at[n], to)
        n += 1

    for f in (0, 1):
        for side in (0, 1):
            to, back, b = ring[f][side], 3 - 2 * side, 2 * f + side
            pair_of = slice(2 * f, 2 * f + 2)
            ag(ag1, (f, side), pv_h.at[pair_of], pvall.at[pair_of, y, x], to)
            ref = pvall.at[b, y, up(x, back)] if f == 0 else pvall.at[b, up(y, back), x]
            ag(ag1f, (f, side), ref, ref, to)
            to = ring[1 - f][side]
            for p in (0, 1):
                ref = pvall.at[2 * f + p, y] if f == 0 else pvall.at[2 * f + p, :, x]
                ag(ag2, (f, side, p), ref, ref, to)
            ref = pvall.at[b, up(y, back)] if f == 0 else pvall.at[b, :, up(x, back)]
            ag(ag2f, (f, side), ref, ref, to)

    def each(msgs, act, *p):
        for f in (0, 1):
            for side in (0, 1):
                getattr(msgs[(f, side, *p)], act)()

    def am(k, passed):
        rows = pl.ds(pl.multiple_of(128 * core + 64 * k, 64), 64)
        src, to, m = (ampb.at[rows], (g_core, w), 2 + k) if passed else (ah.at[1 - zh, rows], (g_chip, w_far), k)
        return send(src, ampb.at[rows], am_s.at[m], am_r.at[m], to)

    def geo(s):
        f, k = lax.rem(s, 2), s // 2
        q = jnp.where(f == 0, x, y)
        right = dev(up(y, f), zh, up(x, 1 - f))
        left = dev(up(y, 4 - f), zh, up(x, 3 + f))
        return f, k, q, right, left

    def rs(s, m):
        _, _, q, right, left = geo(s)
        src, dst, to = {
            0: (part.at[s, up(q, 2), 0:32], r1.at[s, 0], right),
            1: (part.at[s, up(q, 2), 32:64], r1.at[s, 1], left),
            2: (part.at[s, up(q, 1), 32:64], r2.at[s, 0], right),
            3: (part.at[s, up(q, 3), 0:32], r2.at[s, 1], left),
            4: (t3.at[s, 0], r3.at[s, 0], right),
            5: (t3.at[s, 1], r3.at[s, 1], left),
        }[m]
        return send(src, dst, rs_s.at[s, m], rs_r.at[s, m], to)

    def st(f, m):
        right = dev(up(y, 1 - f), zh, up(x, f))
        left = dev(up(y, 3 + f), zh, up(x, 4 - f))
        src, dst, to = {
            0: (s1.at[f, 0, 0:32], u1.at[f, 0], right),
            1: (s1.at[f, 0, 32:64], u1.at[f, 1], left),
            2: (s1.at[f, 1, 32:64], u2.at[f, 0], right),
            3: (s1.at[f, 2, 0:32], u2.at[f, 1], left),
            4: (v3.at[f, 0], u3.at[f, 0], right),
            5: (v3.at[f, 1], u3.at[f, 1], left),
        }[m]
        return send(src, dst, st_s.at[f, m], st_r.at[f, m], to)

    def middle(s):
        _, _, q, _, _ = geo(s)
        rs(s, 0).wait_recv()
        t3[s, 0] = (part[s, up(q, 1), 0:32].astype(F32) + r1[s, 0].astype(F32)).astype(BF)
        rs(s, 4).start()
        rs(s, 1).wait_recv()
        t3[s, 1] = (part[s, up(q, 3), 32:64].astype(F32) + r1[s, 1].astype(F32)).astype(BF)
        rs(s, 5).start()

    def first_sum(s):
        q = geo(s)[2]
        for m in (2, 3, 4, 5):
            rs(s, m).wait_recv()
        lo = part[s, q, 0:32].astype(F32) + r3[s, 0].astype(F32) + r2[s, 1].astype(F32)
        hi = part[s, q, 32:64].astype(F32) + r2[s, 0].astype(F32) + r3[s, 1].astype(F32)
        return lo, hi

    def finish(s):
        f, k = lax.rem(s, 2), s // 2
        lo, hi = first_sum(s)
        s1[f, k, 0:32] = lo.astype(BF)
        s1[f, k, 32:64] = hi.astype(BF)

        @pl.when(k == 0)
        def _():
            st(f, 0).start()
            st(f, 1).start()

        @pl.when(k == 1)
        def _():
            st(f, 2).start()

        @pl.when(k == 2)
        def _():
            st(f, 3).start()

    def gen(s):
        f, k = lax.rem(s, 2), s // 2
        off = jnp.where(k == 0, 2, jnp.where(k == 1, 1, jnp.where(k == 2, 3, 0)))
        for j in range(4):
            c0 = (1 - f) * (128 * up(y, off) + 16 * j) + f * (128 * j + 64 + 16 * up(x, off))
            ob = orb[pl.ds(pl.multiple_of(c0, 16), 16), :]
            for a in range(4):
                pair[j * 64 + a * 16 : j * 64 + a * 16 + 16, :] = rowsb[a] * ob

    def mm(s, t):
        acc = jnp.dot(pair[...], fit[:, t * NT : (t + 1) * NT], preferred_element_type=F32)
        part[s, :, :, t * NT : (t + 1) * NT] = acc.astype(BF).reshape(4, 64, NT)

    l_rows.wait()
    for a in range(4):
        rowsb[a] = jnp.broadcast_to(rows_v[a : a + 1, :], (16, ng))
    piece(0, 0).wait()
    gen(jnp.int32(0))
    pl.semaphore_wait(barrier, 35)
    each(ag1, "start")
    l_amp.wait()
    low = lax.broadcasted_iota(jnp.int32, (1, 1, 128), 2) < 64

    @pl.loop(0, 16)
    def _(i):
        rows = pl.ds(pl.multiple_of(i * 16, 16), 16)
        for m in (0, 1):
            lo = amp[rows, :, 256 * m : 256 * m + 128]
            hi = amp[rows, :, 256 * m + 128 : 256 * m + 256]
            lanes = slice(128 * m, 128 * m + 128)
            ah[0, rows, :, lanes] = jnp.where(low, lo, pltpu.roll(hi, 64, 2))
            ah[1, rows, :, lanes] = jnp.where(low, pltpu.roll(lo, 64, 2), hi)

    for k in (0, 1):
        am(k, 0).start()
    for d in (1, 2, 3):
        piece(d, 0).start()
    for d in range(4):
        piece(d, 1).start()
    for t in range(4):
        fit_tile(t).wait()
    for t in range(tiles):
        mm(0, t)
        if t == max(0, tiles - 2):
            each(ag1, "wait_recv")
            each(ag1f, "start")
    for m in range(4):
        rs(0, m).start()
    for d in (1, 2, 3):
        piece(d, 0).wait()
    for d in range(4):
        piece(d, 1).wait()

    @pl.loop(1, 8)
    def _(s):
        gen(s)
        for t in range(tiles):
            mm(s, t)
        @pl.when(s >= 2)
        def _():
            middle(s - 2)

        for m in range(4):
            rs(s, m).start()

        @pl.when(s == 3)
        def _():
            l_pv.wait()
            each(ag1f, "wait_recv")
            for side in (0, 1):
                ag2[1, side, 0].start()

        @pl.when(s == 4)
        def _():
            for side in (0, 1):
                ag2[0, side, 0].start()

        @pl.when(s == 6)
        def _():
            am(0, 0).wait_recv()
            am(0, 1).start()

        @pl.when(s >= 4)
        def _():
            finish(s - 4)


    def third(f, side):
        st(f, side).wait_recv()
        half = slice(32 * side, 32 * side + 32)
        v3[f, side] = (s1[f, 1 + side, half].astype(F32) + u1[f, side].astype(F32)).astype(BF)
        st(f, 4 + side).start()

    def turn(src, dst, lo, hi):
        @pl.loop(lo, hi, step=2)
        def _(i):
            for k in (0, 1):
                rows = pl.ds(pl.multiple_of((i + k) * 16, 16), 16)
                turned = jnp.dot(perm[...], src[rows].reshape(256, 256), preferred_element_type=F32)
                dst[:, rows, :] = turned.astype(BF).reshape(16, 16, 256)

    third(0, 0)
    third(1, 0)
    turn(ah.at[zh], ampt.at[0], 0, 8)
    middle(6)
    finish(4)
    third(0, 1)
    turn(ah.at[zh], ampt.at[0], 8, 16)
    middle(7)
    finish(5)
    third(1, 1)
    each(ag2, "start", 1)
    am(1, 0).wait_recv()
    am(1, 1).start()

    for f in (0, 1):
        lo, hi = first_sum(jnp.int32(6 + f))
        for m in (2, 3, 4, 5):
            st(f, m).wait_recv()
        lo = lo + u3[f, 0].astype(F32) + u2[f, 1].astype(F32)
        hi = hi + u2[f, 0].astype(F32) + u3[f, 1].astype(F32)
        s2[f, 0:32] = lo
        s2[f, 32:64] = hi
        s2b[f, 0:32] = lo.astype(BF)
        s2b[f, 32:64] = hi.astype(BF)
    halves = (slice(0, 32), slice(32, 64))
    zsend = [
        send(s2b.at[1 - zh, v], zr.at[v], z_s.at[k], z_r.at[k], dev(y, 1 - zh, x)) for k, v in enumerate(halves)
    ]
    for c in zsend:
        c.start()

    for k in (0, 1):
        am(k, 1).wait_recv()
    turn(ampb, ampt.at[1], 0, 16)
    each(ag2, "wait_recv", 0)
    each(ag2, "wait_recv", 1)
    each(ag2f, "start")

    mate, cross, twin = (g_chip, w), (g_chip, w_far), (g_core, w)
    ve = []

    def share(ref, to):
        ve.append(send(ref, ref, ve_s.at[len(ve)], ve_r.at[len(ve)], to))
        return ve[-1]

    to_mate, to_cross, to_twin = [], [], []
    for k, v in enumerate(halves):
        zsend[k].wait_recv()
        vall[zh, g, v] = (s2[zh, v] + zr[v].astype(F32)).astype(BF)
        own = vall.at[zh, g, v]
        for sent, to in ((to_mate, mate), (to_cross, cross), (to_twin, twin)):
            sent.append(share(own, to))
            sent[-1].start()
    of_mate = [vall.at[zh, g_chip, v] for v in halves]
    of_cross = [vall.at[1 - zh, g_chip, v] for v in halves]
    of_far = [vall.at[1 - zh, g, v] for v in halves]
    far = [share(of_cross[0], mate), share(of_mate[1], cross)]
    twin_mate = [share(r, twin) for r in of_mate]
    twin_cross = [share(r, twin) for r in of_cross]
    twin_far = [share(r, twin) for r in of_far]

    to_mate[0].wait_recv()
    twin_mate[0].start()
    to_cross[0].wait_recv()
    far[0].start()
    twin_cross[0].start()
    to_mate[1].wait_recv()
    far[1].start()
    twin_mate[1].start()
    to_cross[1].wait_recv()
    twin_cross[1].start()
    for c in (*to_twin, *twin_mate):
        c.wait_recv()

    nt = (((1,), (1,)), ((), ()))

    def rungs(z):
        vperm[...] = jnp.dot(perm[...], vall[z].reshape(256, na), preferred_element_type=F32).astype(BF)
        for b in range(4):
            rung = lax.dot_general(vperm[...], pvall[b].reshape(256, na), nt, preferred_element_type=F32)
            rg[:, b * 16 : b * 16 + 16, :] = rung.astype(BF).reshape(16, 16, 256)

    def ladder(k):
        acc = jnp.zeros((256, 64), F32)
        for c in range(16):
            acc += lax.dot_general(ampt[k, c], rg[c], nt, preferred_element_type=F32)
        return acc.reshape(32, 8, 64)

    each(ag2f, "wait_recv")
    rungs(zh)
    for k in (0, 1):
        far[k].wait_recv()
        twin_far[k].start()
    lp[:, :, 0:64] = ladder(0)
    lp[:, :, 64:128] = jnp.zeros((32, 8, 64), F32)
    for c in (*twin_cross, *twin_far):
        c.wait_recv()
    rungs(1 - zh)
    lp[:, :, 0:64] += ladder(1)

    def fn(j):
        to = lax.rem(w + j, 32)
        return send(lp.at[to], lr.at[j], fn_s.at[j], fn_r.at[j], (g, to))

    @pl.loop(1, 32)
    def _(j):
        fn(j).start()

    total = lp[w]
    for j in range(1, 32):
        fn(j).wait_recv()
    for j in range(1, 32):
        total += lr[j]
    fr[g] = total

    def fg(j):
        return send(fr.at[g], fr.at[g], fg_s.at[j], fg_r.at[j], (lax.rem(g + j, 4), w))

    for j in (1, 2, 3):
        fg(j).start()
    for j in (1, 2, 3):
        fg(j).wait_recv()
    rr = lax.broadcasted_iota(jnp.int32, (128, 64), 0)
    cc = lax.broadcasted_iota(jnp.int32, (128, 64), 1)
    res = jnp.zeros((8, 64), F32)
    for p in range(4):
        pick = (lax.rem(rr, 16) == g * 4 + cc // 16) & (p * 4 + rr // 16 == lax.rem(cc, 16))
        res += jnp.dot(
            fr[p], jnp.where(pick, jnp.float32(1), jnp.float32(0)),
            precision=lax.Precision.HIGHEST, preferred_element_type=F32,
        )
    for a in range(4):
        out_ref[:, a, :] = res[:, 16 * a : 16 * a + 16]

    for msgs in (ag1, ag1f, ag2, ag2f):
        for c in msgs.values():
            c.wait_send()
    for f in (0, 1):
        for m in range(6):
            st(f, m).wait_send()

    @pl.loop(0, 8)
    def _(s):
        for m in range(6):
            rs(s, m).wait_send()

    for k in (0, 1):
        am(k, 0).wait_send()
        am(k, 1).wait_send()
    for c in (*zsend, *ve):
        c.wait_send()

    @pl.loop(1, 32)
    def _(j):
        fn(j).wait_send()

    for j in (1, 2, 3):
        fg(j).wait_send()


def local(row_orbitals, orbitals, fitting, partner_vertex, amplitudes):
    ng, na = fitting.shape
    dma = pltpu.SemaphoreType.DMA
    half = (32, na)
    return pl.pallas_call(
        kernel,
        out_shape=jax.ShapeDtypeStruct((8, 4, 16), F32),
        in_specs=[pl.BlockSpec(memory_space=pl.ANY)] * 5,
        out_specs=pl.BlockSpec(memory_space=pltpu.VMEM),
        scratch_shapes=[
            pltpu.VMEM((4, ng), BF),
            pltpu.VMEM((4, 16, ng), BF),
            pltpu.VMEM((512, ng), BF),
            pltpu.VMEM((ng, na), BF),
            pltpu.VMEM((256, ng), BF),
            pltpu.VMEM((8, 4, 64, na), BF),
            pltpu.VMEM((8, 2, *half), BF),
            pltpu.VMEM((8, 2, *half), BF),
            pltpu.VMEM((8, 2, *half), BF),
            pltpu.VMEM((8, 2, *half), BF),
            pltpu.VMEM((2, 4, 64, na), BF),
            pltpu.VMEM((2, 2, *half), BF),
            pltpu.VMEM((2, 2, *half), BF),
            pltpu.VMEM((2, 2, *half), BF),
            pltpu.VMEM((2, 2, *half), BF),
            pltpu.VMEM((2, 64, na), F32),
            pltpu.VMEM((2, 64, na), BF),
            pltpu.VMEM((64, na), BF),
            pltpu.VMEM((2, 4, 64, na), BF),
            pltpu.VMEM((256, na), BF),
            pltpu.VMEM((4, 4, 4, 16, na), BF),
            pltpu.VMEM((256, 16, 512), BF),
            pltpu.VMEM((2, 256, 16, 256), BF),
            pltpu.VMEM((256, 16, 256), BF),
            pltpu.VMEM((2, 16, 256, 256), BF),
            pltpu.VMEM((16, 64, 256), BF),
            pltpu.VMEM((32, 8, 128), F32),
            pltpu.VMEM((32, 8, 128), F32),
            pltpu.VMEM((4, 8, 128), F32),
            pltpu.VMEM((256, 256), BF),
            dma((15,)),
            dma((20,)), dma((20,)),
            dma((8, 6)), dma((8, 6)),
            dma((2, 6)), dma((2, 6)),
            dma((2,)), dma((2,)),
            dma((14,)), dma((14,)),
            dma((4,)), dma((4,)),
            dma((32,)), dma((32,)),
            dma((4,)), dma((4,)),
        ],
        compiler_params=pltpu.CompilerParams(
            collective_id=0, has_side_effects=True, vmem_limit_bytes=60 * 1024 * 1024
        ),
    )(row_orbitals, orbitals, fitting, partner_vertex, amplitudes)


def solution(mesh):
    in_specs = (P("grp", "pw"), P(None, "pw"), P("pw", None), P("grp", "pw", None), P(None, "pw", None))
    return jax.shard_map(
        local, mesh=mesh, in_specs=in_specs, out_specs=P("pw", "grp", None), check_vma=False
    )
```

```python
import jax
import jax.numpy as jnp
from jax import lax
from jax.experimental import pallas as pl
from jax.experimental.pallas import tpu as pltpu
from jax.sharding import PartitionSpec as P

MESH = pl.DeviceIdType.MESH
BF = jnp.bfloat16
F32 = jnp.float32
NT = 256


def kernel(
    rows_h, orb_h, fit_h, pv_h, amp_h, out_ref,
    rows_v, rowsb, orb, fit, pair, part, r1, r2, r3, t3, s1, u1, u2, u3, v3, s2b, zr,
    vall, vperm, pvall, amp, ah, ampb, ampt, rg, lp, lr, fr, perm,
    ld, ag_s, ag_r, rs_s, rs_r, st_s, st_r, z_s, z_r, ve_s, ve_r, am_s, am_r, fn_s, fn_r, fg_s, fg_r,
):
    g = lax.axis_index("grp")
    w = lax.axis_index("pw")
    y, zh, x = w // 8, lax.rem(w // 4, 2), lax.rem(w, 4)
    ng = rows_v.shape[1]
    na = fit.shape[1]
    core = lax.rem(g, 2)
    g_core, g_chip = g + 1 - 2 * core, lax.rem(g + 2, 4)
    w_far = w + 4 - 8 * zh

    def dev(yy, zz, xx):
        return (g, yy * 8 + zz * 4 + xx)

    def up(v, by=1):
        return lax.rem(v + by, 4)

    def send(src, dst, ss, rs, to):
        return pltpu.make_async_remote_copy(
            src_ref=src, dst_ref=dst, send_sem=ss, recv_sem=rs, device_id=to, device_id_type=MESH
        )

    barrier = pltpu.get_barrier_semaphore()

    @pl.loop(1, 32)
    def _(j):
        pl.semaphore_signal(barrier, inc=1, device_id=(g, lax.rem(w + j, 32)), device_id_type=MESH)

    @pl.loop(1, 4)
    def _(j):
        pl.semaphore_signal(barrier, inc=1, device_id=(lax.rem(g + j, 4), w), device_id_type=MESH)

    pl.semaphore_signal(barrier, inc=1, device_id=(g_chip, w_far), device_id_type=MESH)

    def piece(d, h):
        rows = pl.ds(pl.multiple_of(128 * d + 64 * (h * zh + (1 - h) * (1 - zh)), 64), 64)
        return pltpu.make_async_copy(orb_h.at[rows, :], orb.at[rows, :], ld.at[7 + 4 * h + d])

    def fit_tile(t):
        rows = slice(t * (ng // 4), (t + 1) * (ng // 4))
        return pltpu.make_async_copy(fit_h.at[rows], fit.at[rows], ld.at[3 + t])

    tiles = na // NT
    l_rows = pltpu.make_async_copy(rows_h, rows_v, ld.at[0])
    l_amp = pltpu.make_async_copy(amp_h, amp, ld.at[1])
    l_pv = pltpu.make_async_copy(pv_h, pvall.at[:, y, x], ld.at[2])
    for c in (l_rows, l_amp, *(piece(d, 0) for d in range(4)), *(fit_tile(t) for t in range(4)), l_pv):
        c.start()

    ring = {0: (dev(y, zh, up(x)), dev(y, zh, up(x, 3))), 1: (dev(up(y), zh, x), dev(up(y, 3), zh, x))}
    ag1, ag1f, ag2, ag2f = {}, {}, {}, {}
    n = 0

    def ag(into, key, src, ref, to):
        nonlocal n
        into[key] = send(src, ref, ag_s.at[n], ag_r.at[n], to)
        n += 1

    for f in (0, 1):
        for side in (0, 1):
            to, back, b = ring[f][side], 3 - 2 * side, 2 * f + side
            pair_of = slice(2 * f, 2 * f + 2)
            own = pv_h.at[pair_of]
            ag(ag1, (f, side), own, pvall.at[pair_of, y, x], to)
            ref = pvall.at[b, y, up(x, back)] if f == 0 else pvall.at[b, up(y, back), x]
            ag(ag1f, (f, side), ref, ref, to)
            to = ring[1 - f][side]
            for d in range(4):
                ref = pvall.at[pair_of, y, up(x, d)] if f == 0 else pvall.at[pair_of, up(y, d), x]
                ag(ag2, (f, side, d), own if d == 0 else ref, ref, to)
            ref = pvall.at[b, up(y, back)] if f == 0 else pvall.at[b, :, up(x, back)]
            ag(ag2f, (f, side), ref, ref, to)

    def each(msgs, act, *p):
        for f in (0, 1):
            for side in (0, 1):
                getattr(msgs[(f, side, *p)], act)()

    def am(k, passed):
        rows = pl.ds(pl.multiple_of(128 * core + 64 * k, 64), 64)
        src, to, m = (ampb.at[rows], (g_core, w), 2 + k) if passed else (ah.at[1 - zh, rows], (g_chip, w_far), k)
        return send(src, ampb.at[rows], am_s.at[m], am_r.at[m], to)

    place = (x, y)

    def rs(s, e, m):
        q, (right, left) = place[e], ring[e]
        src, dst, to = {
            0: lambda: (part.at[s, e, up(q, 2), 0:16], r1.at[s, e, 0], right),
            1: lambda: (part.at[s, e, up(q, 2), 16:32], r1.at[s, e, 1], left),
            2: lambda: (part.at[s, e, up(q, 1), 16:32], r2.at[s, e, 0], right),
            3: lambda: (part.at[s, e, up(q, 3), 0:16], r2.at[s, e, 1], left),
            4: lambda: (t3.at[s, e, 0], r3.at[s, e, 0], right),
            5: lambda: (t3.at[s, e, 1], r3.at[s, e, 1], left),
        }[m]()
        return send(src, dst, rs_s.at[s, e, m], rs_r.at[s, e, m], to)

    def st(h, e, m):
        right, left = ring[1 - e]
        src, dst, to = {
            0: lambda: (s1.at[h, e, 0, 0:16], u1.at[h, e, 0], right),
            1: lambda: (s1.at[h, e, 0, 16:32], u1.at[h, e, 1], left),
            2: lambda: (s1.at[h, e, 1, 16:32], u2.at[h, e, 0], right),
            3: lambda: (s1.at[h, e, 2, 0:16], u2.at[h, e, 1], left),
            4: lambda: (v3.at[h, e, 0], u3.at[h, e, 0], right),
            5: lambda: (v3.at[h, e, 1], u3.at[h, e, 1], left),
        }[m]()
        return send(src, dst, st_s.at[h, e, m], st_r.at[h, e, m], to)

    def sends(s):
        for m in range(4):
            for e in (0, 1):
                rs(s, e, m).start()

    def middle(s):
        for e in (0, 1):
            for side in (0, 1):
                half = slice(16 * side, 16 * side + 16)
                rs(s, e, side).wait_recv()
                mine = part[s, e, up(place[e], 1 + 2 * side), half].astype(F32)
                t3[s, e, side] = (mine + r1[s, e, side].astype(F32)).astype(BF)
                rs(s, e, 4 + side).start()

    def first_sum(s, e):
        for m in (2, 3, 4, 5):
            rs(s, e, m).wait_recv()
        q = place[e]
        lo = part[s, e, q, 0:16].astype(F32) + r3[s, e, 0].astype(F32) + r2[s, e, 1].astype(F32)
        hi = part[s, e, q, 16:32].astype(F32) + r2[s, e, 0].astype(F32) + r3[s, e, 1].astype(F32)
        return lo, hi

    def finish(s, h, k):
        for e in (0, 1):
            lo, hi = first_sum(s, e)
            s1[h, e, k, 0:16] = lo.astype(BF)
            s1[h, e, k, 16:32] = hi.astype(BF)
            for m in ((0, 1), (2,), (3,))[k]:
                st(h, e, m).start()

    def third(h, side):
        half = slice(16 * side, 16 * side + 16)
        for e in (0, 1):
            st(h, e, side).wait_recv()
            v3[h, e, side] = (s1[h, e, 1 + side, half].astype(F32) + u1[h, e, side].astype(F32)).astype(BF)
            st(h, e, 4 + side).start()

    def last_sum(h, e):
        lo, hi = first_sum(4 * h + 3, e)
        for m in (2, 3, 4, 5):
            st(h, e, m).wait_recv()
        lo = lo + u3[h, e, 0].astype(F32) + u2[h, e, 1].astype(F32)
        hi = hi + u2[h, e, 0].astype(F32) + u3[h, e, 1].astype(F32)
        return lo, hi

    zsend = [
        send(s2b.at[e], zr.at[e], z_s.at[e], z_r.at[e], dev(y, 1 - zh, x)) for e in (0, 1)
    ]

    def gen(s):
        h, k = s // 4, lax.rem(s, 4)
        off = jnp.where(k == 0, 2, jnp.where(k == 1, 1, jnp.where(k == 2, 3, 0)))
        z64 = 64 * (h * zh + (1 - h) * (1 - zh))
        for e in (0, 1):
            for j in range(4):
                c0 = 128 * up(y, off) + 16 * j if e == 0 else 128 * j + 16 * up(x, off)
                ob = orb[pl.ds(pl.multiple_of(c0 + z64, 16), 16), :]
                for a in (0, 1):
                    row = 128 * e + 32 * j + 16 * a
                    pair[row : row + 16, :] = rowsb[2 * e + a] * ob

    def mm(s, t):
        acc = jnp.dot(pair[...], fit[:, t * NT : (t + 1) * NT], preferred_element_type=F32)
        part[s, :, :, :, t * NT : (t + 1) * NT] = acc.astype(BF).reshape(2, 4, 32, NT)

    pl.semaphore_wait(barrier, 35)
    each(ag1, "start")
    each(ag2, "start", 0)
    ii = lax.broadcasted_iota(jnp.int32, (256, 256), 0)
    jj = lax.broadcasted_iota(jnp.int32, (256, 256), 1)
    perm[...] = jnp.where(
        jj == lax.rem(ii, 16) * 16 + ii // 16, jnp.float32(1), jnp.float32(0)
    ).astype(BF)
    l_rows.wait()
    for a in range(4):
        rowsb[a] = jnp.broadcast_to(rows_v[a : a + 1, :], (16, ng))
    l_amp.wait()
    low = lax.broadcasted_iota(jnp.int32, (1, 1, 128), 2) < 64

    @pl.loop(0, 16)
    def _(i):
        rows = pl.ds(pl.multiple_of(i * 16, 16), 16)
        for m in (0, 1):
            lo = amp[rows, :, 256 * m : 256 * m + 128]
            hi = amp[rows, :, 256 * m + 128 : 256 * m + 256]
            lanes = slice(128 * m, 128 * m + 128)
            ah[0, rows, :, lanes] = jnp.where(low, lo, pltpu.roll(hi, 64, 2))
            ah[1, rows, :, lanes] = jnp.where(low, pltpu.roll(lo, 64, 2), hi)

    for k in (0, 1):
        am(k, 0).start()
    for d in range(4):
        piece(d, 1).start()
    for d in range(4):
        piece(d, 0).wait()
    for t in range(4):
        fit_tile(t).wait()

    @pl.loop(0, 8)
    def _(s):
        gen(s)
        for t in range(tiles):
            mm(s, t)
        @pl.when(s >= 2)
        def _():
            middle(s - 2)

        sends(s)

        @pl.when(s == 0)
        def _():
            each(ag1, "wait_recv")
            each(ag1f, "start")
            each(ag2, "start", 1)
            for d in range(4):
                piece(d, 1).wait()

        @pl.when(s == 1)
        def _():
            each(ag2, "start", 3)

        @pl.when(s == 6)
        def _():
            am(0, 0).wait_recv()
            am(0, 1).start()

        @pl.when(s == 4)
        def _():
            finish(0, 0, 0)

        @pl.when(s == 5)
        def _():
            finish(1, 0, 1)

        @pl.when(s == 6)
        def _():
            third(0, 0)
            finish(2, 0, 2)
            third(0, 1)


    middle(6)
    for e in (0, 1):
        lo, hi = last_sum(0, e)
        s2b[e, 0:16] = lo.astype(BF)
        s2b[e, 16:32] = hi.astype(BF)
        zsend[e].start()
    finish(4, 1, 0)

    def turn(src, dst, lo, hi):
        @pl.loop(lo, hi, step=2)
        def _(i):
            for k in (0, 1):
                rows = pl.ds(pl.multiple_of((i + k) * 16, 16), 16)
                turned = jnp.dot(perm[...], src[rows].reshape(256, 256), preferred_element_type=F32)
                dst[:, rows, :] = turned.astype(BF).reshape(16, 16, 256)

    turn(ah.at[zh], ampt.at[0], 0, 16)
    middle(7)
    finish(5, 1, 1)
    third(1, 0)
    finish(6, 1, 2)
    third(1, 1)
    each(ag1f, "wait_recv")
    each(ag2, "start", 2)
    am(1, 0).wait_recv()
    am(1, 1).start()

    mate, cross, twin = (g_chip, w), (g_chip, w_far), (g_core, w)
    ve = []

    def share(ref, to):
        ve.append(send(ref, ref, ve_s.at[len(ve)], ve_r.at[len(ve)], to))
        return ve[-1]

    to_mate, to_cross, to_twin = [], [], []
    halves = (slice(0, 32), slice(32, 64))
    for e, v in enumerate(halves):
        lo, hi = last_sum(1, e)
        zsend[e].wait_recv()
        vall[zh, g, 32 * e : 32 * e + 16] = (lo + zr[e, 0:16].astype(F32)).astype(BF)
        vall[zh, g, 32 * e + 16 : 32 * e + 32] = (hi + zr[e, 16:32].astype(F32)).astype(BF)
        own = vall.at[zh, g, v]
        for sent, to in ((to_mate, mate), (to_cross, cross), (to_twin, twin)):
            sent.append(share(own, to))
            sent[-1].start()
    of_mate = [vall.at[zh, g_chip, v] for v in halves]
    of_cross = [vall.at[1 - zh, g_chip, v] for v in halves]
    of_far = [vall.at[1 - zh, g, v] for v in halves]
    far = [share(of_cross[0], mate), share(of_mate[1], cross)]
    twin_mate = [share(r, twin) for r in of_mate]
    twin_cross = [share(r, twin) for r in of_cross]
    twin_far = [share(r, twin) for r in of_far]

    for k in (0, 1):
        am(k, 1).wait_recv()
    turn(ampb, ampt.at[1], 0, 16)
    l_pv.wait()
    for d in range(4):
        each(ag2, "wait_recv", d)
    each(ag2f, "start")
    to_mate[0].wait_recv()
    twin_mate[0].start()
    to_cross[0].wait_recv()
    far[0].start()
    twin_cross[0].start()
    to_mate[1].wait_recv()
    far[1].start()
    twin_mate[1].start()
    to_cross[1].wait_recv()
    twin_cross[1].start()
    for c in (*to_twin, *twin_mate):
        c.wait_recv()

    nt = (((1,), (1,)), ((), ()))

    def rungs(z):
        vperm[...] = jnp.dot(perm[...], vall[z].reshape(256, na), preferred_element_type=F32).astype(BF)
        for b in range(4):
            rung = lax.dot_general(vperm[...], pvall[b].reshape(256, na), nt, preferred_element_type=F32)
            rg[:, b * 16 : b * 16 + 16, :] = rung.astype(BF).reshape(16, 16, 256)

    def ladder(k):
        acc = jnp.zeros((256, 64), F32)
        for c in range(16):
            acc += lax.dot_general(ampt[k, c], rg[c], nt, preferred_element_type=F32)
        return acc.reshape(32, 8, 64)

    each(ag2f, "wait_recv")
    rungs(zh)
    for k in (0, 1):
        far[k].wait_recv()
        twin_far[k].start()
    lp[:, :, 0:64] = ladder(0)
    lp[:, :, 64:128] = jnp.zeros((32, 8, 64), F32)
    for c in (*twin_cross, *twin_far):
        c.wait_recv()
    rungs(1 - zh)
    lp[:, :, 0:64] += ladder(1)

    def fn(j):
        to = lax.rem(w + j, 32)
        return send(lp.at[to], lr.at[j], fn_s.at[j], fn_r.at[j], (g, to))

    @pl.loop(1, 32)
    def _(j):
        fn(j).start()

    total = lp[w]
    for j in range(1, 32):
        fn(j).wait_recv()
    for j in range(1, 32):
        total += lr[j]
    fr[g] = total

    def fg(j):
        return send(fr.at[g], fr.at[g], fg_s.at[j], fg_r.at[j], (lax.rem(g + j, 4), w))

    for j in (1, 2, 3):
        fg(j).start()
    for j in (1, 2, 3):
        fg(j).wait_recv()
    rr = lax.broadcasted_iota(jnp.int32, (128, 64), 0)
    cc = lax.broadcasted_iota(jnp.int32, (128, 64), 1)
    res = jnp.zeros((8, 64), F32)
    for p in range(4):
        pick = (lax.rem(rr, 16) == g * 4 + cc // 16) & (p * 4 + rr // 16 == lax.rem(cc, 16))
        res += jnp.dot(
            fr[p], jnp.where(pick, jnp.float32(1), jnp.float32(0)),
            precision=lax.Precision.HIGHEST, preferred_element_type=F32,
        )
    for a in range(4):
        out_ref[:, a, :] = res[:, 16 * a : 16 * a + 16]

    for msgs in (ag1, ag1f, ag2, ag2f):
        for c in msgs.values():
            c.wait_send()
    for e in (0, 1):
        for m in range(6):
            for h in (0, 1):
                st(h, e, m).wait_send()

    @pl.loop(0, 8)
    def _(s):
        for e in (0, 1):
            for m in range(6):
                rs(s, e, m).wait_send()

    for k in (0, 1):
        am(k, 0).wait_send()
        am(k, 1).wait_send()
    for c in (*zsend, *ve):
        c.wait_send()

    @pl.loop(1, 32)
    def _(j):
        fn(j).wait_send()

    for j in (1, 2, 3):
        fg(j).wait_send()


def local(row_orbitals, orbitals, fitting, partner_vertex, amplitudes):
    ng, na = fitting.shape
    dma = pltpu.SemaphoreType.DMA
    return pl.pallas_call(
        kernel,
        out_shape=jax.ShapeDtypeStruct((8, 4, 16), F32),
        in_specs=[pl.BlockSpec(memory_space=pl.ANY)] * 5,
        out_specs=pl.BlockSpec(memory_space=pltpu.VMEM),
        scratch_shapes=[
            pltpu.VMEM((4, ng), BF),
            pltpu.VMEM((4, 16, ng), BF),
            pltpu.VMEM((512, ng), BF),
            pltpu.VMEM((ng, na), BF),
            pltpu.VMEM((256, ng), BF),
            pltpu.VMEM((8, 2, 4, 32, na), BF),
            pltpu.VMEM((8, 2, 2, 16, na), BF),
            pltpu.VMEM((8, 2, 2, 16, na), BF),
            pltpu.VMEM((8, 2, 2, 16, na), BF),
            pltpu.VMEM((8, 2, 2, 16, na), BF),
            pltpu.VMEM((2, 2, 4, 32, na), BF),
            pltpu.VMEM((2, 2, 2, 16, na), BF),
            pltpu.VMEM((2, 2, 2, 16, na), BF),
            pltpu.VMEM((2, 2, 2, 16, na), BF),
            pltpu.VMEM((2, 2, 2, 16, na), BF),
            pltpu.VMEM((2, 32, na), BF),
            pltpu.VMEM((2, 32, na), BF),
            pltpu.VMEM((2, 4, 64, na), BF),
            pltpu.VMEM((256, na), BF),
            pltpu.VMEM((4, 4, 4, 16, na), BF),
            pltpu.VMEM((256, 16, 512), BF),
            pltpu.VMEM((2, 256, 16, 256), BF),
            pltpu.VMEM((256, 16, 256), BF),
            pltpu.VMEM((2, 16, 256, 256), BF),
            pltpu.VMEM((16, 64, 256), BF),
            pltpu.VMEM((32, 8, 128), F32),
            pltpu.VMEM((32, 8, 128), F32),
            pltpu.VMEM((4, 8, 128), F32),
            pltpu.VMEM((256, 256), BF),
            dma((15,)),
            dma((28,)), dma((28,)),
            dma((8, 2, 6)), dma((8, 2, 6)),
            dma((2, 2, 6)), dma((2, 2, 6)),
            dma((2,)), dma((2,)),
            dma((14,)), dma((14,)),
            dma((4,)), dma((4,)),
            dma((32,)), dma((32,)),
            dma((4,)), dma((4,)),
        ],
        compiler_params=pltpu.CompilerParams(
            collective_id=0, has_side_effects=True, vmem_limit_bytes=60 * 1024 * 1024
        ),
    )(row_orbitals, orbitals, fitting, partner_vertex, amplitudes)


def solution(mesh):
    in_specs = (P("grp", "pw"), P(None, "pw"), P("pw", None), P("grp", "pw", None), P(None, "pw", None))
    return jax.shard_map(
        local, mesh=mesh, in_specs=in_specs, out_specs=P("pw", "grp", None), check_vma=False
    )
```

```python
import jax
import jax.numpy as jnp
from jax import lax
from jax.experimental import pallas as pl
from jax.experimental.pallas import tpu as pltpu
from jax.sharding import PartitionSpec as P

MESH = pl.DeviceIdType.MESH
BF = jnp.bfloat16
F32 = jnp.float32
NT = 256


def kernel(
    rows_h, orb_h, fit_h, pv_h, amp_h, out_ref,
    rows_v, rowsb, orb, fit, pair, part, r1, r2, r3, t3, s1, u1, u2, u3, v3, s2b, zr,
    vall, vperm, pvall, amp, ah, ampb, ampt, rg, lp, lr, fo, fr, pick, perm,
    ld, ag_s, ag_r, rs_s, rs_r, st_s, st_r, z_s, z_r, ve_s, ve_r, am_s, am_r, fn_s, fn_r, fg_s, fg_r,
):
    g = lax.axis_index("grp")
    w = lax.axis_index("pw")
    y, zh, x = w // 8, lax.rem(w // 4, 2), lax.rem(w, 4)
    ng = rows_v.shape[1]
    na = fit.shape[1]
    core = lax.rem(g, 2)
    g_core, g_chip = g + 1 - 2 * core, lax.rem(g + 2, 4)
    w_far = w + 4 - 8 * zh

    def dev(yy, zz, xx):
        return (g, yy * 8 + zz * 4 + xx)

    def up(v, by=1):
        return lax.rem(v + by, 4)

    def send(src, dst, ss, rs, to):
        return pltpu.make_async_remote_copy(
            src_ref=src, dst_ref=dst, send_sem=ss, recv_sem=rs, device_id=to, device_id_type=MESH
        )

    def piece(d, h):
        rows = pl.ds(pl.multiple_of(128 * d + 64 * (h * zh + (1 - h) * (1 - zh)), 64), 64)
        return pltpu.make_async_copy(orb_h.at[rows, :], orb.at[rows, :], ld.at[7 + 4 * h + d])

    def fit_tile(t):
        rows = slice(t * (ng // 4), (t + 1) * (ng // 4))
        return pltpu.make_async_copy(fit_h.at[rows], fit.at[rows], ld.at[3 + t])

    tiles = na // NT
    l_rows = pltpu.make_async_copy(rows_h, rows_v, ld.at[0])

    def l_amp(k):
        rows = pl.ds(pl.multiple_of(128 * (k + core - 2 * k * core), 128), 128)
        return pltpu.make_async_copy(amp_h.at[rows], amp.at[rows], ld.at[1 + 14 * k])

    l_pv = pltpu.make_async_copy(pv_h, pvall.at[:, y, x], ld.at[2])
    for c in (l_rows, l_amp(0), *(piece(d, 0) for d in range(4)), *(fit_tile(t) for t in range(4)), l_pv):
        c.start()

    barrier = pltpu.get_barrier_semaphore()

    @pl.loop(1, 16)
    def _(j):
        peer = dev(up(y, j // 4), zh, up(x, lax.rem(j, 4)))
        pl.semaphore_signal(barrier, inc=1, device_id=peer, device_id_type=MESH)

    @pl.loop(1, 8)
    def _(j):
        peer = (lax.rem(g + j, 4), w + (j // 4) * (4 - 8 * zh))
        pl.semaphore_signal(barrier, inc=1, device_id=peer, device_id_type=MESH)

    ring = {0: (dev(y, zh, up(x)), dev(y, zh, up(x, 3))), 1: (dev(up(y), zh, x), dev(up(y, 3), zh, x))}
    ag1, ag1f, ag2, ag2f = {}, {}, {}, {}
    n = 0

    def ag(into, key, src, ref, to):
        nonlocal n
        into[key] = send(src, ref, ag_s.at[n], ag_r.at[n], to)
        n += 1

    for f in (0, 1):
        for side in (0, 1):
            to, back, b = ring[f][side], 3 - 2 * side, 2 * f + side
            pair_of = slice(2 * f, 2 * f + 2)
            own = pv_h.at[pair_of]
            ag(ag1, (f, side), own, pvall.at[pair_of, y, x], to)
            ref = pvall.at[b, y, up(x, back)] if f == 0 else pvall.at[b, up(y, back), x]
            ag(ag1f, (f, side), ref, ref, to)
            to = ring[1 - f][side]
            for d in range(4):
                ref = pvall.at[pair_of, y, up(x, d)] if f == 0 else pvall.at[pair_of, up(y, d), x]
                ag(ag2, (f, side, d), own if d == 0 else ref, ref, to)
            for d in range(4):
                ref = pvall.at[b, up(y, back), up(x, d)] if f == 0 else pvall.at[b, up(y, d), up(x, back)]
                ag(ag2f, (f, side, d), ref, ref, to)

    def each(msgs, act, *p):
        for f in (0, 1):
            for side in (0, 1):
                getattr(msgs[(f, side, *p)], act)()

    def am(k, passed):
        rows = pl.ds(pl.multiple_of(128 * core + 64 * k, 64), 64)
        src, to, m = (ampb.at[rows], (g_core, w), 2 + k) if passed else (ah.at[64 * k : 64 * k + 64], (g_chip, w_far), k)
        return send(src, ampb.at[rows], am_s.at[m], am_r.at[m], to)

    place = (x, y)

    def rs(s, e, m):
        q, (right, left) = place[e], ring[e]
        src, dst, to = {
            0: lambda: (part.at[s, e, up(q, 2), 0:16], r1.at[s, e, 0], right),
            1: lambda: (part.at[s, e, up(q, 2), 16:32], r1.at[s, e, 1], left),
            2: lambda: (part.at[s, e, up(q, 1), 16:32], r2.at[s, e, 0], right),
            3: lambda: (part.at[s, e, up(q, 3), 0:16], r2.at[s, e, 1], left),
            4: lambda: (t3.at[s, e, 0], r3.at[s, e, 0], right),
            5: lambda: (t3.at[s, e, 1], r3.at[s, e, 1], left),
        }[m]()
        return send(src, dst, rs_s.at[s, e, m], rs_r.at[s, e, m], to)

    def st(h, e, m):
        right, left = ring[1 - e]
        src, dst, to = {
            0: lambda: (s1.at[h, e, 0, 0:16], u1.at[h, e, 0], right),
            1: lambda: (s1.at[h, e, 0, 16:32], u1.at[h, e, 1], left),
            2: lambda: (s1.at[h, e, 1, 16:32], u2.at[h, e, 0], right),
            3: lambda: (s1.at[h, e, 2, 0:16], u2.at[h, e, 1], left),
            4: lambda: (v3.at[h, e, 0], u3.at[h, e, 0], right),
            5: lambda: (v3.at[h, e, 1], u3.at[h, e, 1], left),
        }[m]()
        return send(src, dst, st_s.at[h, e, m], st_r.at[h, e, m], to)

    def sends(s, ms):
        for m in ms:
            for e in (0, 1):
                rs(s, e, m).start()

    def middle(s):
        for e in (0, 1):
            for side in (0, 1):
                half = slice(16 * side, 16 * side + 16)
                rs(s, e, side).wait_recv()
                mine = part[s, e, up(place[e], 1 + 2 * side), half].astype(F32)
                t3[s, e, side] = (mine + r1[s, e, side].astype(F32)).astype(BF)
                rs(s, e, 4 + side).start()

    def first_sum(s, e):
        for m in (2, 3, 4, 5):
            rs(s, e, m).wait_recv()
        q = place[e]
        lo = part[s, e, q, 0:16].astype(F32) + r3[s, e, 0].astype(F32) + r2[s, e, 1].astype(F32)
        hi = part[s, e, q, 16:32].astype(F32) + r2[s, e, 0].astype(F32) + r3[s, e, 1].astype(F32)
        return lo, hi

    def finish(s, h, k):
        for e in (0, 1):
            lo, hi = first_sum(s, e)
            s1[h, e, k, 0:16] = lo.astype(BF)
            s1[h, e, k, 16:32] = hi.astype(BF)
            for m in ((0, 1), (2,), (3,))[k]:
                st(h, e, m).start()

    def third(h, side):
        half = slice(16 * side, 16 * side + 16)
        for e in (0, 1):
            st(h, e, side).wait_recv()
            v3[h, e, side] = (s1[h, e, 1 + side, half].astype(F32) + u1[h, e, side].astype(F32)).astype(BF)
            st(h, e, 4 + side).start()

    def last_sum(h, e):
        lo, hi = first_sum(4 * h + 3, e)
        for m in (2, 3, 4, 5):
            st(h, e, m).wait_recv()
        lo = lo + u3[h, e, 0].astype(F32) + u2[h, e, 1].astype(F32)
        hi = hi + u2[h, e, 0].astype(F32) + u3[h, e, 1].astype(F32)
        return lo, hi

    zsend = [
        send(s2b.at[e], zr.at[e], z_s.at[e], z_r.at[e], dev(y, 1 - zh, x)) for e in (0, 1)
    ]

    def gen(s):
        h, k = s // 4, lax.rem(s, 4)
        off = jnp.where(k == 0, 2, jnp.where(k == 1, 1, jnp.where(k == 2, 3, 0)))
        z64 = 64 * (h * zh + (1 - h) * (1 - zh))
        for e in (0, 1):
            for j in range(4):
                c0 = 128 * up(y, off) + 16 * j if e == 0 else 128 * j + 16 * up(x, off)
                ob = orb[pl.ds(pl.multiple_of(c0 + z64, 16), 16), :]
                for a in (0, 1):
                    row = 128 * e + 32 * j + 16 * a
                    pair[row : row + 16, :] = rowsb[2 * e + a] * ob

    def mm(s, t):
        acc = jnp.dot(pair[...], fit[:, t * NT : (t + 1) * NT], preferred_element_type=F32)
        part[s, :, :, :, t * NT : (t + 1) * NT] = acc.astype(BF).reshape(2, 4, 32, NT)

    pl.semaphore_wait(barrier, 22)
    each(ag1, "start")
    each(ag2, "start", 0)
    ii = lax.broadcasted_iota(jnp.int32, (256, 256), 0)
    jj = lax.broadcasted_iota(jnp.int32, (256, 256), 1)
    perm[...] = jnp.where(
        jj == lax.rem(ii, 16) * 16 + ii // 16, jnp.float32(1), jnp.float32(0)
    ).astype(BF)
    l_rows.wait()
    for a in range(4):
        rowsb[a] = jnp.broadcast_to(rows_v[a : a + 1, :], (16, ng))
    low = lax.broadcasted_iota(jnp.int32, (1, 1, 128), 2) < 64

    def lanes_of(rows, plane):
        first, parts = plane == 0, []
        for m in (0, 1):
            lo = amp[rows, :, 256 * m : 256 * m + 128]
            hi = amp[rows, :, 256 * m + 128 : 256 * m + 256]
            lo = jnp.where(first, lo, pltpu.roll(lo, 64, 2))
            hi = jnp.where(first, pltpu.roll(hi, 64, 2), hi)
            parts.append(jnp.where(low, lo, hi))
        return jnp.concatenate(parts, axis=2)

    l_amp(0).wait()
    @pl.loop(0, 8)
    def _(i):
        rows = pl.ds(pl.multiple_of(128 * core + i * 16, 16), 16)
        ah[pl.ds(pl.multiple_of(i * 16, 16), 16)] = lanes_of(rows, 1 - zh)

    for k in (0, 1):
        am(k, 0).start()
    for d in range(4):
        piece(d, 1).start()
    l_amp(1).start()
    for d in range(4):
        piece(d, 0).wait()
    for t in range(4):
        fit_tile(t).wait()

    @pl.loop(0, 8)
    def _(s):
        gen(s)
        for t in range(tiles):
            mm(s, t)
        sends(s, (0, 1))

        @pl.when(s >= 2)
        def _():
            middle(s - 2)

        sends(s, (2, 3))

        @pl.when(s == 0)
        def _():
            each(ag1, "wait_recv")
            each(ag1f, "start")
            each(ag2, "start", 1)
            for d in range(4):
                piece(d, 1).wait()

        @pl.when(s == 6)
        def _():
            am(0, 0).wait_recv()
            am(0, 1).start()

        @pl.when(s == 4)
        def _():
            finish(0, 0, 0)

        @pl.when(s == 5)
        def _():
            finish(1, 0, 1)

        @pl.when(s == 6)
        def _():
            third(0, 0)
            finish(2, 0, 2)
            third(0, 1)


    def turn(block, dst, lo, hi):
        @pl.loop(lo, hi, step=2)
        def _(i):
            for k in (0, 1):
                rows = pl.ds(pl.multiple_of((i + k) * 16, 16), 16)
                turned = jnp.dot(perm[...], block(rows).reshape(256, 256), preferred_element_type=F32)
                dst[:, rows, :] = turned.astype(BF).reshape(16, 16, 256)

    def own_lanes(rows):
        return lanes_of(rows, zh)

    finish(4, 1, 0)
    middle(6)
    l_amp(1).wait()
    turn(own_lanes, ampt.at[0], 0, 8)
    am(1, 0).wait_recv()
    am(1, 1).start()
    for e in (0, 1):
        lo, hi = last_sum(0, e)
        s2b[e, 0:16] = lo.astype(BF)
        s2b[e, 16:32] = hi.astype(BF)
        zsend[e].start()
    middle(7)
    finish(5, 1, 1)
    third(1, 0)
    finish(6, 1, 2)
    third(1, 1)
    each(ag1f, "wait_recv")
    for d in (3, 2):
        each(ag2, "start", d)
    for d in (0, 1):
        each(ag2, "wait_recv", d)
        each(ag2f, "start", d)
    turn(own_lanes, ampt.at[0], 8, 16)

    for k in (0, 1):
        am(k, 1).wait_recv()
    turn(lambda rows: ampb[rows], ampt.at[1], 0, 16)
    mate, cross, twin = (g_chip, w), (g_chip, w_far), (g_core, w)
    ve = []

    def share(ref, to):
        ve.append(send(ref, ref, ve_s.at[len(ve)], ve_r.at[len(ve)], to))
        return ve[-1]

    to_mate, to_cross, to_twin = [], [], []
    halves = (slice(0, 32), slice(32, 64))
    for e, v in enumerate(halves):
        lo, hi = last_sum(1, e)
        zsend[e].wait_recv()
        vall[zh, g, 32 * e : 32 * e + 16] = (lo + zr[e, 0:16].astype(F32)).astype(BF)
        vall[zh, g, 32 * e + 16 : 32 * e + 32] = (hi + zr[e, 16:32].astype(F32)).astype(BF)
        own = vall.at[zh, g, v]
        for sent, to in ((to_mate, mate), (to_cross, cross), (to_twin, twin)):
            sent.append(share(own, to))
            sent[-1].start()
    of_mate = [vall.at[zh, g_chip, v] for v in halves]
    of_cross = [vall.at[1 - zh, g_chip, v] for v in halves]
    of_far = [vall.at[1 - zh, g, v] for v in halves]
    far = [share(of_cross[0], mate), share(of_mate[1], cross)]
    twin_mate = [share(r, twin) for r in of_mate]
    twin_cross = [share(r, twin) for r in of_cross]
    twin_far = [share(r, twin) for r in of_far]

    for d in (3, 2):
        each(ag2, "wait_recv", d)
        each(ag2f, "start", d)
    to_mate[0].wait_recv()
    twin_mate[0].start()
    to_cross[0].wait_recv()
    far[0].start()
    twin_cross[0].start()
    to_mate[1].wait_recv()
    far[1].start()
    twin_mate[1].start()
    to_cross[1].wait_recv()
    twin_cross[1].start()
    for c in (*to_twin, *twin_mate):
        c.wait_recv()

    nt = (((1,), (1,)), ((), ()))

    def rungs(z):
        vperm[...] = jnp.dot(perm[...], vall[z].reshape(256, na), preferred_element_type=F32).astype(BF)
        for b in range(4):
            rung = lax.dot_general(vperm[...], pvall[b].reshape(256, na), nt, preferred_element_type=F32)
            rg[:, b * 16 : b * 16 + 16, :] = rung.astype(BF).reshape(16, 16, 256)

    def ladder(k):
        acc = jnp.zeros((256, 64), F32)
        for c in range(16):
            acc += lax.dot_general(ampt[k, c], rg[c], nt, preferred_element_type=F32)
        return acc.reshape(4, 2, 4, 8, 64)

    l_pv.wait()
    for d in range(4):
        each(ag2f, "wait_recv", d)
    rungs(zh)
    for k in (0, 1):
        far[k].wait_recv()
        twin_far[k].start()
    lp[..., 0:64] = ladder(0)
    lp[..., 64:128] = jnp.zeros((4, 2, 4, 8, 64), F32)
    for c in (*twin_cross, *twin_far):
        c.wait_recv()
    rungs(1 - zh)
    lp[..., 0:64] += ladder(1)

    def fn(j):
        yy, xx = up(y, j // 4), up(x, lax.rem(j, 4))
        return send(lp.at[yy, :, xx], lr.at[j], fn_s.at[j], fn_r.at[j], dev(yy, zh, xx))

    @pl.loop(1, 16)
    def _(j):
        fn(16 - j).start()

    for msgs in (ag1, ag1f, ag2, ag2f):
        for c in msgs.values():
            c.wait_send()
    for e in (0, 1):
        for m in range(6):
            for h in (0, 1):
                st(h, e, m).wait_send()

    @pl.loop(0, 8)
    def _(s):
        for e in (0, 1):
            for m in range(6):
                rs(s, e, m).wait_send()

    for k in (0, 1):
        am(k, 0).wait_send()
        am(k, 1).wait_send()
    for c in (*zsend, *ve):
        c.wait_send()

    rr = lax.broadcasted_iota(jnp.int32, (128, 64), 0)
    cc = lax.broadcasted_iota(jnp.int32, (128, 64), 1)
    for p in range(4):
        chosen = (lax.rem(rr, 16) == g * 4 + cc // 16) & (p * 4 + rr // 16 == lax.rem(cc, 16))
        pick[p] = jnp.where(chosen, jnp.float32(1), jnp.float32(0))

    total = lp[y, :, x]
    for j in range(1, 16):
        fn(j).wait_recv()
    for j in range(1, 16):
        total += lr[j]
    fo[...] = total

    def fg(j):
        far_z, gg = j // 4, lax.rem(g + j, 4)
        zz = zh + far_z - 2 * zh * far_z
        return send(fo.at[zz], fr.at[far_z, g], fg_s.at[j], fg_r.at[j], (gg, y * 8 + zz * 4 + x))

    for j in (6, 5, 7, 2, 4, 3, 1):
        fg(j).start()
    fr[0, g] = fo[zh]
    for j in range(1, 8):
        fg(j).wait_recv()
    res = jnp.zeros((8, 64), F32)
    for p in range(4):
        res += jnp.dot(fr[0, p] + fr[1, p], pick[p], precision=lax.Precision.HIGHEST, preferred_element_type=F32)
    for a in range(4):
        out_ref[:, a, :] = res[:, 16 * a : 16 * a + 16]

    @pl.loop(1, 16)
    def _(j):
        fn(j).wait_send()

    for j in range(1, 8):
        fg(j).wait_send()


def local(row_orbitals, orbitals, fitting, partner_vertex, amplitudes):
    ng, na = fitting.shape
    dma = pltpu.SemaphoreType.DMA
    return pl.pallas_call(
        kernel,
        out_shape=jax.ShapeDtypeStruct((8, 4, 16), F32),
        in_specs=[pl.BlockSpec(memory_space=pl.ANY)] * 5,
        out_specs=pl.BlockSpec(memory_space=pltpu.VMEM),
        scratch_shapes=[
            pltpu.VMEM((4, ng), BF),
            pltpu.VMEM((4, 16, ng), BF),
            pltpu.VMEM((512, ng), BF),
            pltpu.VMEM((ng, na), BF),
            pltpu.VMEM((256, ng), BF),
            pltpu.VMEM((8, 2, 4, 32, na), BF),
            pltpu.VMEM((8, 2, 2, 16, na), BF),
            pltpu.VMEM((8, 2, 2, 16, na), BF),
            pltpu.VMEM((8, 2, 2, 16, na), BF),
            pltpu.VMEM((8, 2, 2, 16, na), BF),
            pltpu.VMEM((2, 2, 4, 32, na), BF),
            pltpu.VMEM((2, 2, 2, 16, na), BF),
            pltpu.VMEM((2, 2, 2, 16, na), BF),
            pltpu.VMEM((2, 2, 2, 16, na), BF),
            pltpu.VMEM((2, 2, 2, 16, na), BF),
            pltpu.VMEM((2, 32, na), BF),
            pltpu.VMEM((2, 32, na), BF),
            pltpu.VMEM((2, 4, 64, na), BF),
            pltpu.VMEM((256, na), BF),
            pltpu.VMEM((4, 4, 4, 16, na), BF),
            pltpu.VMEM((256, 16, 512), BF),
            pltpu.VMEM((128, 16, 256), BF),
            pltpu.VMEM((256, 16, 256), BF),
            pltpu.VMEM((2, 16, 256, 256), BF),
            pltpu.VMEM((16, 64, 256), BF),
            pltpu.VMEM((4, 2, 4, 8, 128), F32),
            pltpu.VMEM((16, 2, 8, 128), F32),
            pltpu.VMEM((2, 8, 128), F32),
            pltpu.VMEM((2, 4, 8, 128), F32),
            pltpu.VMEM((4, 128, 64), F32),
            pltpu.VMEM((256, 256), BF),
            dma((16,)),
            dma((40,)), dma((40,)),
            dma((8, 2, 6)), dma((8, 2, 6)),
            dma((2, 2, 6)), dma((2, 2, 6)),
            dma((2,)), dma((2,)),
            dma((14,)), dma((14,)),
            dma((4,)), dma((4,)),
            dma((16,)), dma((16,)),
            dma((8,)), dma((8,)),
        ],
        compiler_params=pltpu.CompilerParams(
            collective_id=0, has_side_effects=True, vmem_limit_bytes=60 * 1024 * 1024
        ),
    )(row_orbitals, orbitals, fitting, partner_vertex, amplitudes)


def solution(mesh):
    in_specs = (P("grp", "pw"), P(None, "pw"), P("pw", None), P("grp", "pw", None), P(None, "pw", None))
    return jax.shard_map(
        local, mesh=mesh, in_specs=in_specs, out_specs=P("pw", "grp", None), check_vma=False
    )
```

```python
import jax
import jax.numpy as jnp
from jax import lax
from jax.experimental import pallas as pl
from jax.experimental.pallas import tpu as pltpu
from jax.sharding import PartitionSpec as P

MESH = pl.DeviceIdType.MESH
BF = jnp.bfloat16
F32 = jnp.float32
NT = 256


def kernel(
    rows_h, orb_h, fit_h, pv_h, amp_h, out_ref,
    rows_v, rowsb, orb, fit, pair, part, r1, r2, r3, t3, s1, u1, u2, u3, v3, s2b, zr,
    vall, vperm, pvall, amp, ah, ampb, ampt, rg, lacc, lp, lr, fo, fr, pick, perm,
    ld, ag_s, ag_r, rs_s, rs_r, st_s, st_r, z_s, z_r, ve_s, ve_r, am_s, am_r, fn_s, fn_r, fg_s, fg_r,
):
    g = lax.axis_index("grp")
    w = lax.axis_index("pw")
    y, zh, x = w // 8, lax.rem(w // 4, 2), lax.rem(w, 4)
    ng = rows_v.shape[1]
    na = fit.shape[1]
    core = lax.rem(g, 2)
    g_core, g_chip = g + 1 - 2 * core, lax.rem(g + 2, 4)
    w_far = w + 4 - 8 * zh

    def dev(yy, zz, xx):
        return (g, yy * 8 + zz * 4 + xx)

    def up(v, by=1):
        return lax.rem(v + by, 4)

    def send(src, dst, ss, rs, to):
        return pltpu.make_async_remote_copy(
            src_ref=src, dst_ref=dst, send_sem=ss, recv_sem=rs, device_id=to, device_id_type=MESH
        )

    def piece(d, h):
        rows = pl.ds(pl.multiple_of(128 * d + 64 * (h * zh + (1 - h) * (1 - zh)), 64), 64)
        return pltpu.make_async_copy(orb_h.at[rows, :], orb.at[rows, :], ld.at[7 + 4 * h + d])

    def fit_tile(t):
        rows = slice(t * (ng // 4), (t + 1) * (ng // 4))
        return pltpu.make_async_copy(fit_h.at[rows], fit.at[rows], ld.at[3 + t])

    tiles = na // NT
    l_rows = pltpu.make_async_copy(rows_h, rows_v, ld.at[0])

    def l_amp(k):
        rows = pl.ds(pl.multiple_of(64 * lax.rem(g + 2 + k, 4), 64), 64)
        return pltpu.make_async_copy(amp_h.at[rows], amp.at[rows], ld.at[14 + k if k else 1])

    l_pv = pltpu.make_async_copy(pv_h, pvall.at[:, y, x], ld.at[2])
    for c in (l_rows, l_amp(0), *(piece(d, 0) for d in range(4)), *(fit_tile(t) for t in range(4)), l_pv):
        c.start()

    barrier = pltpu.get_barrier_semaphore()

    @pl.loop(1, 16)
    def _(j):
        peer = dev(up(y, j // 4), zh, up(x, lax.rem(j, 4)))
        pl.semaphore_signal(barrier, inc=1, device_id=peer, device_id_type=MESH)

    @pl.loop(1, 8)
    def _(j):
        peer = (lax.rem(g + j, 4), w + (j // 4) * (4 - 8 * zh))
        pl.semaphore_signal(barrier, inc=1, device_id=peer, device_id_type=MESH)

    ring = {0: (dev(y, zh, up(x)), dev(y, zh, up(x, 3))), 1: (dev(up(y), zh, x), dev(up(y, 3), zh, x))}
    ag1, ag1f, ag2, ag2f = {}, {}, {}, {}
    n = 0

    def ag(into, key, src, ref, to):
        nonlocal n
        into[key] = send(src, ref, ag_s.at[n], ag_r.at[n], to)
        n += 1

    for f in (0, 1):
        for side in (0, 1):
            to, back, b = ring[f][side], 3 - 2 * side, 2 * f + side
            pair_of = slice(2 * f, 2 * f + 2)
            own = pv_h.at[pair_of]
            ag(ag1, (f, side), own, pvall.at[pair_of, y, x], to)
            ref = pvall.at[b, y, up(x, back)] if f == 0 else pvall.at[b, up(y, back), x]
            ag(ag1f, (f, side), ref, ref, to)
            to = ring[1 - f][side]
            for d in range(4):
                ref = pvall.at[pair_of, y, up(x, d)] if f == 0 else pvall.at[pair_of, up(y, d), x]
                ag(ag2, (f, side, d), own if d == 0 else ref, ref, to)
            for d in range(4):
                ref = pvall.at[b, up(y, back), up(x, d)] if f == 0 else pvall.at[b, up(y, d), up(x, back)]
                ag(ag2f, (f, side, d), ref, ref, to)

    def each(msgs, act, *p):
        for f in (0, 1):
            for side in (0, 1):
                getattr(msgs[(f, side, *p)], act)()

    def quarter(q):
        return pl.ds(pl.multiple_of(64 * q, 64), 64)

    mine, theirs = g, lax.rem(g + 2, 4)

    def am(k):
        src, rows, to = (
            (ah, theirs, (g_chip, w_far)),
            (ampb.at[quarter(mine)], mine, (g_chip, w)),
            (ampb.at[quarter(mine)], mine, (g_core, w)),
            (ampb.at[quarter(theirs)], theirs, (g_core, w)),
        )[k]
        return send(src, ampb.at[quarter(rows)], am_s.at[k], am_r.at[k], to)

    place = (x, y)

    def rs(s, e, m):
        q, (right, left) = place[e], ring[e]
        src, dst, to = {
            0: lambda: (part.at[s, e, up(q, 2), 0:16], r1.at[s, e, 0], right),
            1: lambda: (part.at[s, e, up(q, 2), 16:32], r1.at[s, e, 1], left),
            2: lambda: (part.at[s, e, up(q, 1), 16:32], r2.at[s, e, 0], right),
            3: lambda: (part.at[s, e, up(q, 3), 0:16], r2.at[s, e, 1], left),
            4: lambda: (t3.at[s, e, 0], r3.at[s, e, 0], right),
            5: lambda: (t3.at[s, e, 1], r3.at[s, e, 1], left),
        }[m]()
        return send(src, dst, rs_s.at[s, e, m], rs_r.at[s, e, m], to)

    def st(h, e, m):
        right, left = ring[1 - e]
        src, dst, to = {
            0: lambda: (s1.at[h, e, 0, 0:16], u1.at[h, e, 0], right),
            1: lambda: (s1.at[h, e, 0, 16:32], u1.at[h, e, 1], left),
            2: lambda: (s1.at[h, e, 1, 16:32], u2.at[h, e, 0], right),
            3: lambda: (s1.at[h, e, 2, 0:16], u2.at[h, e, 1], left),
            4: lambda: (v3.at[h, e, 0], u3.at[h, e, 0], right),
            5: lambda: (v3.at[h, e, 1], u3.at[h, e, 1], left),
        }[m]()
        return send(src, dst, st_s.at[h, e, m], st_r.at[h, e, m], to)

    def sends(s, ms):
        for m in ms:
            for e in (0, 1):
                rs(s, e, m).start()

    def middle(s):
        for e in (0, 1):
            for side in (0, 1):
                half = slice(16 * side, 16 * side + 16)
                rs(s, e, side).wait_recv()
                mine = part[s, e, up(place[e], 1 + 2 * side), half].astype(F32)
                t3[s, e, side] = (mine + r1[s, e, side].astype(F32)).astype(BF)
                rs(s, e, 4 + side).start()

    def first_sum(s, e):
        for m in (2, 3, 4, 5):
            rs(s, e, m).wait_recv()
        q = place[e]
        lo = part[s, e, q, 0:16].astype(F32) + r3[s, e, 0].astype(F32) + r2[s, e, 1].astype(F32)
        hi = part[s, e, q, 16:32].astype(F32) + r2[s, e, 0].astype(F32) + r3[s, e, 1].astype(F32)
        return lo, hi

    def finish(s, h, k):
        for e in (0, 1):
            lo, hi = first_sum(s, e)
            s1[h, e, k, 0:16] = lo.astype(BF)
            s1[h, e, k, 16:32] = hi.astype(BF)
            for m in ((0, 1), (2,), (3,))[k]:
                st(h, e, m).start()

    def third(h, side):
        half = slice(16 * side, 16 * side + 16)
        for e in (0, 1):
            st(h, e, side).wait_recv()
            v3[h, e, side] = (s1[h, e, 1 + side, half].astype(F32) + u1[h, e, side].astype(F32)).astype(BF)
            st(h, e, 4 + side).start()

    def last_sum(h, e):
        lo, hi = first_sum(4 * h + 3, e)
        for m in (2, 3, 4, 5):
            st(h, e, m).wait_recv()
        lo = lo + u3[h, e, 0].astype(F32) + u2[h, e, 1].astype(F32)
        hi = hi + u2[h, e, 0].astype(F32) + u3[h, e, 1].astype(F32)
        return lo, hi

    zsend = [
        send(s2b.at[e], zr.at[e], z_s.at[e], z_r.at[e], dev(y, 1 - zh, x)) for e in (0, 1)
    ]

    def gen(s):
        h, k = s // 4, lax.rem(s, 4)
        off = jnp.where(k == 0, 2, jnp.where(k == 1, 1, jnp.where(k == 2, 3, 0)))
        z64 = 64 * (h * zh + (1 - h) * (1 - zh))
        for e in (0, 1):
            for j in range(4):
                c0 = 128 * up(y, off) + 16 * j if e == 0 else 128 * j + 16 * up(x, off)
                ob = orb[pl.ds(pl.multiple_of(c0 + z64, 16), 16), :]
                for a in (0, 1):
                    row = 128 * e + 32 * j + 16 * a
                    pair[row : row + 16, :] = rowsb[2 * e + a] * ob

    def mm(s, t):
        acc = jnp.dot(pair[...], fit[:, t * NT : (t + 1) * NT], preferred_element_type=F32)
        part[s, :, :, :, t * NT : (t + 1) * NT] = acc.astype(BF).reshape(2, 4, 32, NT)

    pl.semaphore_wait(barrier, 22)
    each(ag1, "start")
    each(ag2, "start", 0)
    ii = lax.broadcasted_iota(jnp.int32, (256, 256), 0)
    jj = lax.broadcasted_iota(jnp.int32, (256, 256), 1)
    perm[...] = jnp.where(
        jj == lax.rem(ii, 16) * 16 + ii // 16, jnp.float32(1), jnp.float32(0)
    ).astype(BF)
    l_rows.wait()
    for a in range(4):
        rowsb[a] = jnp.broadcast_to(rows_v[a : a + 1, :], (16, ng))
    low = lax.broadcasted_iota(jnp.int32, (1, 1, 128), 2) < 64

    def lanes_of(rows, plane):
        first, parts = plane == 0, []
        for m in (0, 1):
            lo = amp[rows, :, 256 * m : 256 * m + 128]
            hi = amp[rows, :, 256 * m + 128 : 256 * m + 256]
            lo = jnp.where(first, lo, pltpu.roll(lo, 64, 2))
            hi = jnp.where(first, pltpu.roll(hi, 64, 2), hi)
            parts.append(jnp.where(low, lo, hi))
        return jnp.concatenate(parts, axis=2)

    l_amp(0).wait()
    @pl.loop(0, 4)
    def _(i):
        rows = pl.ds(pl.multiple_of(64 * theirs + i * 16, 16), 16)
        ah[pl.ds(pl.multiple_of(i * 16, 16), 16)] = lanes_of(rows, 1 - zh)

    am(0).start()
    for d in range(4):
        piece(d, 1).start()
    for k in (1, 2, 3):
        l_amp(k).start()
    for d in range(4):
        piece(d, 0).wait()
    for t in range(4):
        fit_tile(t).wait()

    @pl.loop(0, 8)
    def _(s):
        gen(s)
        for t in range(tiles):
            mm(s, t)
        sends(s, (0, 1))

        @pl.when(s >= 2)
        def _():
            middle(s - 2)

        sends(s, (2, 3))

        @pl.when(s == 0)
        def _():
            each(ag1, "wait_recv")
            each(ag1f, "start")
            each(ag2, "start", 1)
            for d in range(4):
                piece(d, 1).wait()

        @pl.when(s == 4)
        def _():
            am(0).wait_recv()
            am(1).start()
            am(2).start()

        @pl.when(s == 4)
        def _():
            finish(0, 0, 0)

        @pl.when(s == 5)
        def _():
            finish(1, 0, 1)

        @pl.when(s == 6)
        def _():
            third(0, 0)
            finish(2, 0, 2)
            third(0, 1)


    def turn(block, dst, lo, hi):
        @pl.loop(lo, hi, step=2)
        def _(i):
            for k in (0, 1):
                rows = pl.ds(pl.multiple_of((i + k) * 16, 16), 16)
                turned = jnp.dot(perm[...], block(rows).reshape(256, 256), preferred_element_type=F32)
                dst[:, rows, :] = turned.astype(BF).reshape(16, 16, 256)

    def own_lanes(rows):
        return lanes_of(rows, zh)

    finish(4, 1, 0)
    middle(6)
    for k in (1, 2, 3):
        l_amp(k).wait()
    turn(own_lanes, ampt.at[0], 0, 8)
    for e in (0, 1):
        lo, hi = last_sum(0, e)
        s2b[e, 0:16] = lo.astype(BF)
        s2b[e, 16:32] = hi.astype(BF)
        zsend[e].start()
    middle(7)
    finish(5, 1, 1)
    third(1, 0)
    am(1).wait_recv()
    am(3).start()
    finish(6, 1, 2)
    third(1, 1)
    each(ag1f, "wait_recv")
    for d in (3, 2):
        each(ag2, "start", d)
    for d in (0, 1):
        each(ag2, "wait_recv", d)
        each(ag2f, "start", d)
    turn(own_lanes, ampt.at[0], 8, 16)

    def turn_far():
        am(2).wait_recv()
        am(3).wait_recv()
        turn(lambda rows: ampb[rows], ampt.at[1], 0, 16)

    pl.when(core == 0)(turn_far)
    mate, cross, twin = (g_chip, w), (g_chip, w_far), (g_core, w)
    ve = []

    def share(ref, to):
        ve.append(send(ref, ref, ve_s.at[len(ve)], ve_r.at[len(ve)], to))
        return ve[-1]

    to_mate, to_cross, to_twin = [], [], []
    halves = (slice(0, 32), slice(32, 64))
    for e, v in enumerate(halves):
        lo, hi = last_sum(1, e)
        zsend[e].wait_recv()
        vall[zh, g, 32 * e : 32 * e + 16] = (lo + zr[e, 0:16].astype(F32)).astype(BF)
        vall[zh, g, 32 * e + 16 : 32 * e + 32] = (hi + zr[e, 16:32].astype(F32)).astype(BF)
        own = vall.at[zh, g, v]
        for sent, to in ((to_mate, mate), (to_cross, cross), (to_twin, twin)):
            sent.append(share(own, to))
            sent[-1].start()
    of_mate = [vall.at[zh, g_chip, v] for v in halves]
    of_cross = [vall.at[1 - zh, g_chip, v] for v in halves]
    of_far = [vall.at[1 - zh, g, v] for v in halves]
    far = [share(of_cross[0], mate), share(of_mate[1], cross)]
    twin_mate = [share(r, twin) for r in of_mate]
    twin_cross = [share(r, twin) for r in of_cross]
    twin_far = [share(r, twin) for r in of_far]

    pl.when(core == 1)(turn_far)
    for d in (3, 2):
        each(ag2, "wait_recv", d)
        each(ag2f, "start", d)
    to_mate[0].wait_recv()
    twin_mate[0].start()
    to_cross[0].wait_recv()
    far[0].start()
    twin_cross[0].start()
    to_mate[1].wait_recv()
    far[1].start()
    twin_mate[1].start()
    to_cross[1].wait_recv()
    twin_cross[1].start()
    for c in (*to_twin, *twin_mate):
        c.wait_recv()

    nt = (((1,), (1,)), ((), ()))

    def rungs(z):
        vperm[...] = jnp.dot(perm[...], vall[z].reshape(256, na), preferred_element_type=F32).astype(BF)
        for b in range(4):
            rung = lax.dot_general(vperm[...], pvall[b].reshape(256, na), nt, preferred_element_type=F32)
            rg[:, b * 16 : b * 16 + 16, :] = rung.astype(BF).reshape(16, 16, 256)

    def ladder(k):
        acc = jnp.zeros((256, 64), F32)
        for c in range(16):
            acc += lax.dot_general(ampt[k, c], rg[c], nt, preferred_element_type=F32)
        return acc

    l_pv.wait()
    for d in range(4):
        each(ag2f, "wait_recv", d)
    rungs(zh)
    for k in (0, 1):
        far[k].wait_recv()
        twin_far[k].start()
    lacc[...] = ladder(0)
    for c in (*twin_cross, *twin_far):
        c.wait_recv()
    rungs(1 - zh)
    both = (lacc[...] + ladder(1)).reshape(4, 2, 4, 8, 64)
    lp[..., 0:64] = both[:, 0]
    lp[..., 64:128] = both[:, 1]

    def fn(j):
        yy, xx = up(y, j // 4), up(x, lax.rem(j, 4))
        return send(lp.at[yy, xx], lr.at[j], fn_s.at[j], fn_r.at[j], dev(yy, zh, xx))

    @pl.loop(1, 16)
    def _(j):
        fn(16 - j).start()

    for msgs in (ag1, ag1f, ag2, ag2f):
        for c in msgs.values():
            c.wait_send()
    for e in (0, 1):
        for m in range(6):
            for h in (0, 1):
                st(h, e, m).wait_send()

    @pl.loop(0, 8)
    def _(s):
        for e in (0, 1):
            for m in range(6):
                rs(s, e, m).wait_send()

    for k in range(4):
        am(k).wait_send()
    for c in (*zsend, *ve):
        c.wait_send()

    rr = lax.broadcasted_iota(jnp.int32, (512, 64), 0)
    cc = lax.broadcasted_iota(jnp.int32, (512, 64), 1)
    lane = lax.rem(rr, 128)
    chosen = (lax.rem(lane, 16) == g * 4 + cc // 16) & (lane // 64 == zh)
    chosen = chosen & (rr // 128 * 4 + lax.rem(lane, 64) // 16 == lax.rem(cc, 16))
    pick[...] = jnp.where(chosen, jnp.float32(1), jnp.float32(0))

    total = lp[y, x]
    for j in range(1, 16):
        fn(j).wait_recv()
    for j in range(1, 16):
        total += lr[j]
    fo[...] = total

    def fg(j):
        far_z, gg = j // 4, lax.rem(g + j, 4)
        zz = zh + far_z - 2 * zh * far_z
        return send(fo, fr.at[far_z, g], fg_s.at[j], fg_r.at[j], (gg, y * 8 + zz * 4 + x))

    for j in (6, 5, 7, 2, 4, 3, 1):
        fg(j).start()
    fr[0, g] = total
    for j in range(1, 8):
        fg(j).wait_recv()
    sums = jnp.concatenate([fr[0, p] + fr[1, p] for p in range(4)], axis=1)
    res = jnp.dot(sums, pick[...], precision=lax.Precision.HIGHEST, preferred_element_type=F32)
    for a in range(4):
        out_ref[:, a, :] = res[:, 16 * a : 16 * a + 16]

    @pl.loop(1, 16)
    def _(j):
        fn(j).wait_send()

    for j in range(1, 8):
        fg(j).wait_send()


def local(row_orbitals, orbitals, fitting, partner_vertex, amplitudes):
    ng, na = fitting.shape
    dma = pltpu.SemaphoreType.DMA
    return pl.pallas_call(
        kernel,
        out_shape=jax.ShapeDtypeStruct((8, 4, 16), F32),
        in_specs=[pl.BlockSpec(memory_space=pl.ANY)] * 5,
        out_specs=pl.BlockSpec(memory_space=pltpu.VMEM),
        scratch_shapes=[
            pltpu.VMEM((4, ng), BF),
            pltpu.VMEM((4, 16, ng), BF),
            pltpu.VMEM((512, ng), BF),
            pltpu.VMEM((ng, na), BF),
            pltpu.VMEM((256, ng), BF),
            pltpu.VMEM((8, 2, 4, 32, na), BF),
            pltpu.VMEM((8, 2, 2, 16, na), BF),
            pltpu.VMEM((8, 2, 2, 16, na), BF),
            pltpu.VMEM((8, 2, 2, 16, na), BF),
            pltpu.VMEM((8, 2, 2, 16, na), BF),
            pltpu.VMEM((2, 2, 4, 32, na), BF),
            pltpu.VMEM((2, 2, 2, 16, na), BF),
            pltpu.VMEM((2, 2, 2, 16, na), BF),
            pltpu.VMEM((2, 2, 2, 16, na), BF),
            pltpu.VMEM((2, 2, 2, 16, na), BF),
            pltpu.VMEM((2, 32, na), BF),
            pltpu.VMEM((2, 32, na), BF),
            pltpu.VMEM((2, 4, 64, na), BF),
            pltpu.VMEM((256, na), BF),
            pltpu.VMEM((4, 4, 4, 16, na), BF),
            pltpu.VMEM((256, 16, 512), BF),
            pltpu.VMEM((64, 16, 256), BF),
            pltpu.VMEM((256, 16, 256), BF),
            pltpu.VMEM((2, 16, 256, 256), BF),
            pltpu.VMEM((16, 64, 256), BF),
            pltpu.VMEM((256, 64), F32),
            pltpu.VMEM((4, 4, 8, 128), F32),
            pltpu.VMEM((16, 8, 128), F32),
            pltpu.VMEM((8, 128), F32),
            pltpu.VMEM((2, 4, 8, 128), F32),
            pltpu.VMEM((512, 64), F32),
            pltpu.VMEM((256, 256), BF),
            dma((18,)),
            dma((40,)), dma((40,)),
            dma((8, 2, 6)), dma((8, 2, 6)),
            dma((2, 2, 6)), dma((2, 2, 6)),
            dma((2,)), dma((2,)),
            dma((14,)), dma((14,)),
            dma((4,)), dma((4,)),
            dma((16,)), dma((16,)),
            dma((8,)), dma((8,)),
        ],
        compiler_params=pltpu.CompilerParams(
            collective_id=0, has_side_effects=True, vmem_limit_bytes=60 * 1024 * 1024
        ),
    )(row_orbitals, orbitals, fitting, partner_vertex, amplitudes)


def solution(mesh):
    in_specs = (P("grp", "pw"), P(None, "pw"), P("pw", None), P("grp", "pw", None), P(None, "pw", None))
    return jax.shard_map(
        local, mesh=mesh, in_specs=in_specs, out_specs=P("pw", "grp", None), check_vma=False
    )
```

```python
import jax
import jax.numpy as jnp
from jax import lax
from jax.experimental import pallas as pl
from jax.experimental.pallas import tpu as pltpu
from jax.sharding import PartitionSpec as P

MESH = pl.DeviceIdType.MESH
BF = jnp.bfloat16
F32 = jnp.float32
NT = 256


def kernel(
    rows_h, orb_h, fit_h, pv_h, amp_h, out_ref,
    rows_v, rowsb, orb, fit, pair, part, r1, r2, r3, t3, s1, u1, u2, u3, v3, s2b, zr,
    vall, vperm, pvall, amp, ah, ampb, ampt, rg, lacc, lp, lr, fo, fr, pick, perm,
    ld, ag_s, ag_r, rs_s, rs_r, st_s, st_r, z_s, z_r, ve_s, ve_r, am_s, am_r, fn_s, fn_r, fg_s, fg_r,
):
    g = lax.axis_index("grp")
    w = lax.axis_index("pw")
    y, zh, x = w // 8, lax.rem(w // 4, 2), lax.rem(w, 4)
    ng = rows_v.shape[1]
    na = fit.shape[1]
    core = lax.rem(g, 2)
    g_core, g_chip = g + 1 - 2 * core, lax.rem(g + 2, 4)
    w_far = w + 4 - 8 * zh

    def dev(yy, zz, xx):
        return (g, yy * 8 + zz * 4 + xx)

    def up(v, by=1):
        return lax.rem(v + by, 4)

    def send(src, dst, ss, rs, to):
        return pltpu.make_async_remote_copy(
            src_ref=src, dst_ref=dst, send_sem=ss, recv_sem=rs, device_id=to, device_id_type=MESH
        )

    def piece(d, h):
        rows = pl.ds(pl.multiple_of(128 * d + 64 * (h * zh + (1 - h) * (1 - zh)), 64), 64)
        return pltpu.make_async_copy(orb_h.at[rows, :], orb.at[rows, :], ld.at[7 + 4 * h + d])

    def fit_tile(t):
        rows = slice(t * (ng // 4), (t + 1) * (ng // 4))
        return pltpu.make_async_copy(fit_h.at[rows], fit.at[rows], ld.at[3 + t])

    tiles = na // NT
    l_rows = pltpu.make_async_copy(rows_h, rows_v, ld.at[0])

    def l_amp(k):
        rows = pl.ds(pl.multiple_of(64 * lax.rem(g + 2 + k, 4), 64), 64)
        return pltpu.make_async_copy(amp_h.at[rows], amp.at[rows], ld.at[14 + k if k else 1])

    l_pv = pltpu.make_async_copy(pv_h, pvall.at[:, y, x], ld.at[2])
    for c in (l_rows, l_amp(0), *(piece(d, 0) for d in range(4)), *(fit_tile(t) for t in range(4)), l_pv):
        c.start()

    barrier = pltpu.get_barrier_semaphore()

    @pl.loop(1, 16)
    def _(j):
        peer = dev(up(y, j // 4), zh, up(x, lax.rem(j, 4)))
        pl.semaphore_signal(barrier, inc=1, device_id=peer, device_id_type=MESH)

    @pl.loop(1, 8)
    def _(j):
        peer = (lax.rem(g + j, 4), w + (j // 4) * (4 - 8 * zh))
        pl.semaphore_signal(barrier, inc=1, device_id=peer, device_id_type=MESH)

    ring = {0: (dev(y, zh, up(x)), dev(y, zh, up(x, 3))), 1: (dev(up(y), zh, x), dev(up(y, 3), zh, x))}
    ag1, ag1f, ag2, ag2f = {}, {}, {}, {}
    n = 0

    def ag(into, key, src, ref, to):
        nonlocal n
        into[key] = send(src, ref, ag_s.at[n], ag_r.at[n], to)
        n += 1

    for f in (0, 1):
        for side in (0, 1):
            to, back, b = ring[f][side], 3 - 2 * side, 2 * f + side
            pair_of = slice(2 * f, 2 * f + 2)
            own = pv_h.at[pair_of]
            ag(ag1, (f, side), own, pvall.at[pair_of, y, x], to)
            ref = pvall.at[b, y, up(x, back)] if f == 0 else pvall.at[b, up(y, back), x]
            ag(ag1f, (f, side), ref, ref, to)
            to = ring[1 - f][side]
            for d in range(4):
                ref = pvall.at[pair_of, y, up(x, d)] if f == 0 else pvall.at[pair_of, up(y, d), x]
                ag(ag2, (f, side, d), own if d == 0 else ref, ref, to)
            for d in range(4):
                ref = pvall.at[b, up(y, back), up(x, d)] if f == 0 else pvall.at[b, up(y, d), up(x, back)]
                ag(ag2f, (f, side, d), ref, ref, to)

    def each(msgs, act, *p):
        for f in (0, 1):
            for side in (0, 1):
                getattr(msgs[(f, side, *p)], act)()

    def quarter(q):
        return pl.ds(pl.multiple_of(64 * q, 64), 64)

    mine, theirs = g, lax.rem(g + 2, 4)

    def am(k):
        src, rows, to = (
            (ah, theirs, (g_chip, w_far)),
            (ampb.at[quarter(mine)], mine, (g_chip, w)),
            (ampb.at[quarter(mine)], mine, (g_core, w)),
            (ampb.at[quarter(theirs)], theirs, (g_core, w)),
        )[k]
        return send(src, ampb.at[quarter(rows)], am_s.at[k], am_r.at[k], to)

    place = (x, y)

    def rs(s, e, m):
        q, (right, left) = place[e], ring[e]
        src, dst, to = {
            0: lambda: (part.at[s, e, up(q, 2), 0:16], r1.at[s, e, 0], right),
            1: lambda: (part.at[s, e, up(q, 2), 16:32], r1.at[s, e, 1], left),
            2: lambda: (part.at[s, e, up(q, 1), 16:32], r2.at[s, e, 0], right),
            3: lambda: (part.at[s, e, up(q, 3), 0:16], r2.at[s, e, 1], left),
            4: lambda: (t3.at[s, e, 0], r3.at[s, e, 0], right),
            5: lambda: (t3.at[s, e, 1], r3.at[s, e, 1], left),
        }[m]()
        return send(src, dst, rs_s.at[s, e, m], rs_r.at[s, e, m], to)

    def st(h, e, m):
        right, left = ring[1 - e]
        src, dst, to = {
            0: lambda: (s1.at[h, e, 0, 0:16], u1.at[h, e, 0], right),
            1: lambda: (s1.at[h, e, 0, 16:32], u1.at[h, e, 1], left),
            2: lambda: (s1.at[h, e, 1, 16:32], u2.at[h, e, 0], right),
            3: lambda: (s1.at[h, e, 2, 0:16], u2.at[h, e, 1], left),
            4: lambda: (v3.at[h, e, 0], u3.at[h, e, 0], right),
            5: lambda: (v3.at[h, e, 1], u3.at[h, e, 1], left),
        }[m]()
        return send(src, dst, st_s.at[h, e, m], st_r.at[h, e, m], to)

    def sends(s, ms):
        for m in ms:
            for e in (0, 1):
                rs(s, e, m).start()

    def middle(s):
        for e in (0, 1):
            for side in (0, 1):
                half = slice(16 * side, 16 * side + 16)
                rs(s, e, side).wait_recv()
                mine = part[s, e, up(place[e], 1 + 2 * side), half].astype(F32)
                t3[s, e, side] = (mine + r1[s, e, side].astype(F32)).astype(BF)
                rs(s, e, 4 + side).start()

    def first_sum(s, e):
        for m in (2, 3, 4, 5):
            rs(s, e, m).wait_recv()
        q = place[e]
        lo = part[s, e, q, 0:16].astype(F32) + r3[s, e, 0].astype(F32) + r2[s, e, 1].astype(F32)
        hi = part[s, e, q, 16:32].astype(F32) + r2[s, e, 0].astype(F32) + r3[s, e, 1].astype(F32)
        return lo, hi

    def finish(s, h, k):
        for e in (0, 1):
            lo, hi = first_sum(s, e)
            s1[h, e, k, 0:16] = lo.astype(BF)
            s1[h, e, k, 16:32] = hi.astype(BF)
            for m in ((0, 1), (2,), (3,))[k]:
                st(h, e, m).start()

    def third(h, side):
        half = slice(16 * side, 16 * side + 16)
        for e in (0, 1):
            st(h, e, side).wait_recv()
            v3[h, e, side] = (s1[h, e, 1 + side, half].astype(F32) + u1[h, e, side].astype(F32)).astype(BF)
            st(h, e, 4 + side).start()

    def last_sum(h, e):
        lo, hi = first_sum(4 * h + 3, e)
        for m in (2, 3, 4, 5):
            st(h, e, m).wait_recv()
        lo = lo + u3[h, e, 0].astype(F32) + u2[h, e, 1].astype(F32)
        hi = hi + u2[h, e, 0].astype(F32) + u3[h, e, 1].astype(F32)
        return lo, hi

    zsend = [
        send(s2b.at[e], zr.at[e], z_s.at[e], z_r.at[e], dev(y, 1 - zh, x)) for e in (0, 1)
    ]

    def gen(s):
        h, k = s // 4, lax.rem(s, 4)
        off = jnp.where(k == 0, 2, jnp.where(k == 1, 1, jnp.where(k == 2, 3, 0)))
        z64 = 64 * (h * zh + (1 - h) * (1 - zh))
        for e in (0, 1):
            for j in range(4):
                c0 = 128 * up(y, off) + 16 * j if e == 0 else 128 * j + 16 * up(x, off)
                ob = orb[pl.ds(pl.multiple_of(c0 + z64, 16), 16), :]
                for a in (0, 1):
                    row = 128 * e + 32 * j + 16 * a
                    pair[row : row + 16, :] = rowsb[2 * e + a] * ob

    def mm(s, t):
        acc = jnp.dot(pair[...], fit[:, t * NT : (t + 1) * NT], preferred_element_type=F32)
        part[s, :, :, :, t * NT : (t + 1) * NT] = acc.astype(BF).reshape(2, 4, 32, NT)

    pl.semaphore_wait(barrier, 22)
    each(ag1, "start")
    each(ag2, "start", 0)
    ii = lax.broadcasted_iota(jnp.int32, (256, 256), 0)
    jj = lax.broadcasted_iota(jnp.int32, (256, 256), 1)
    perm[...] = jnp.where(
        jj == lax.rem(ii, 16) * 16 + ii // 16, jnp.float32(1), jnp.float32(0)
    ).astype(BF)
    l_rows.wait()
    for a in range(4):
        rowsb[a] = jnp.broadcast_to(rows_v[a : a + 1, :], (16, ng))
    low = lax.broadcasted_iota(jnp.int32, (1, 1, 128), 2) < 64

    def lanes_of(rows, plane):
        first, parts = plane == 0, []
        for m in (0, 1):
            lo = amp[rows, :, 256 * m : 256 * m + 128]
            hi = amp[rows, :, 256 * m + 128 : 256 * m + 256]
            lo = jnp.where(first, lo, pltpu.roll(lo, 64, 2))
            hi = jnp.where(first, pltpu.roll(hi, 64, 2), hi)
            parts.append(jnp.where(low, lo, hi))
        return jnp.concatenate(parts, axis=2)

    l_amp(0).wait()
    @pl.loop(0, 4)
    def _(i):
        rows = pl.ds(pl.multiple_of(64 * theirs + i * 16, 16), 16)
        ah[pl.ds(pl.multiple_of(i * 16, 16), 16)] = lanes_of(rows, 1 - zh)

    am(0).start()
    for d in range(4):
        piece(d, 1).start()
    for k in (1, 2, 3):
        l_amp(k).start()
    for d in range(4):
        piece(d, 0).wait()
    for t in range(4):
        fit_tile(t).wait()

    @pl.loop(0, 8)
    def _(s):
        gen(s)
        for t in range(tiles):
            mm(s, t)
        sends(s, (0, 1))

        @pl.when(s >= 2)
        def _():
            middle(s - 2)

        @pl.when(s < 7)
        def _():
            sends(s, (2, 3))

        @pl.when(s == 0)
        def _():
            each(ag1, "wait_recv")
            each(ag1f, "start")
            each(ag2, "start", 1)
            for d in range(4):
                piece(d, 1).wait()

        @pl.when(s == 4)
        def _():
            am(0).wait_recv()
            am(1).start()
            am(2).start()

        @pl.when(s == 4)
        def _():
            finish(0, 0, 0)

        @pl.when(s == 5)
        def _():
            finish(1, 0, 1)

        @pl.when(s == 6)
        def _():
            third(0, 0)
            finish(2, 0, 2)
            third(0, 1)


    def turn(block, dst, lo, hi):
        @pl.loop(lo, hi, step=2)
        def _(i):
            for k in (0, 1):
                rows = pl.ds(pl.multiple_of((i + k) * 16, 16), 16)
                turned = jnp.dot(perm[...], block(rows).reshape(256, 256), preferred_element_type=F32)
                dst[:, rows, :] = turned.astype(BF).reshape(16, 16, 256)

    def own_lanes(rows):
        return lanes_of(rows, zh)

    finish(4, 1, 0)
    middle(6)
    sends(jnp.int32(7), (2, 3))
    for k in (1, 2, 3):
        l_amp(k).wait()
    turn(own_lanes, ampt.at[0], 0, 8)
    turn(own_lanes, ampt.at[0], 8, 16)
    for e in (0, 1):
        lo, hi = last_sum(0, e)
        s2b[e, 0:16] = lo.astype(BF)
        s2b[e, 16:32] = hi.astype(BF)
        zsend[e].start()
    middle(7)
    finish(5, 1, 1)
    third(1, 0)
    am(1).wait_recv()
    am(3).start()
    finish(6, 1, 2)
    third(1, 1)
    each(ag1f, "wait_recv")
    for d in (3, 2):
        each(ag2, "start", d)
    for d in (0, 1):
        each(ag2, "wait_recv", d)
        each(ag2f, "start", d)

    def turn_far():
        am(2).wait_recv()
        am(3).wait_recv()
        turn(lambda rows: ampb[rows], ampt.at[1], 0, 16)

    pl.when(core == 0)(turn_far)
    mate, cross, twin = (g_chip, w), (g_chip, w_far), (g_core, w)
    ve = []

    def share(ref, to):
        ve.append(send(ref, ref, ve_s.at[len(ve)], ve_r.at[len(ve)], to))
        return ve[-1]

    to_mate, to_cross, to_twin = [], [], []
    halves = (slice(0, 32), slice(32, 64))
    for e, v in enumerate(halves):
        lo, hi = last_sum(1, e)
        zsend[e].wait_recv()
        vall[zh, g, 32 * e : 32 * e + 16] = (lo + zr[e, 0:16].astype(F32)).astype(BF)
        vall[zh, g, 32 * e + 16 : 32 * e + 32] = (hi + zr[e, 16:32].astype(F32)).astype(BF)
        own = vall.at[zh, g, v]
        for sent, to in ((to_mate, mate), (to_cross, cross), (to_twin, twin)):
            sent.append(share(own, to))
            sent[-1].start()
    of_mate = [vall.at[zh, g_chip, v] for v in halves]
    of_cross = [vall.at[1 - zh, g_chip, v] for v in halves]
    of_far = [vall.at[1 - zh, g, v] for v in halves]
    far = [share(of_cross[0], mate), share(of_mate[1], cross)]
    twin_mate = [share(r, twin) for r in of_mate]
    twin_cross = [share(r, twin) for r in of_cross]
    twin_far = [share(r, twin) for r in of_far]

    pl.when(core == 1)(turn_far)
    for d in (3, 2):
        each(ag2, "wait_recv", d)
        each(ag2f, "start", d)
    to_mate[0].wait_recv()
    twin_mate[0].start()
    to_cross[0].wait_recv()
    far[0].start()
    twin_cross[0].start()
    to_mate[1].wait_recv()
    far[1].start()
    twin_mate[1].start()
    to_cross[1].wait_recv()
    twin_cross[1].start()
    for c in (*to_twin, *twin_mate):
        c.wait_recv()

    nt = (((1,), (1,)), ((), ()))

    def rungs(z):
        vperm[...] = jnp.dot(perm[...], vall[z].reshape(256, na), preferred_element_type=F32).astype(BF)
        for b in range(4):
            rung = lax.dot_general(vperm[...], pvall[b].reshape(256, na), nt, preferred_element_type=F32)
            rg[:, b * 16 : b * 16 + 16, :] = rung.astype(BF).reshape(16, 16, 256)

    def ladder(k):
        acc = jnp.zeros((256, 64), F32)
        for c in range(16):
            acc += lax.dot_general(ampt[k, c], rg[c], nt, preferred_element_type=F32)
        return acc

    l_pv.wait()
    for d in range(4):
        each(ag2f, "wait_recv", d)
    rungs(zh)
    for k in (0, 1):
        far[k].wait_recv()
        twin_far[k].start()
    lacc[...] = ladder(0)
    for c in (*twin_cross, *twin_far):
        c.wait_recv()
    rungs(1 - zh)
    both = (lacc[...] + ladder(1)).reshape(4, 2, 4, 8, 64)
    lp[..., 0:64] = both[:, 0]
    lp[..., 64:128] = both[:, 1]

    def fn(j):
        yy, xx = up(y, j // 4), up(x, lax.rem(j, 4))
        return send(lp.at[yy, xx], lr.at[j], fn_s.at[j], fn_r.at[j], dev(yy, zh, xx))

    @pl.loop(1, 16)
    def _(j):
        fn(16 - j).start()

    for msgs in (ag1, ag1f, ag2, ag2f):
        for c in msgs.values():
            c.wait_send()
    for e in (0, 1):
        for m in range(6):
            for h in (0, 1):
                st(h, e, m).wait_send()

    @pl.loop(0, 8)
    def _(s):
        for e in (0, 1):
            for m in range(6):
                rs(s, e, m).wait_send()

    for k in range(4):
        am(k).wait_send()
    for c in (*zsend, *ve):
        c.wait_send()

    rr = lax.broadcasted_iota(jnp.int32, (512, 64), 0)
    cc = lax.broadcasted_iota(jnp.int32, (512, 64), 1)
    lane = lax.rem(rr, 128)
    chosen = (lax.rem(lane, 16) == g * 4 + cc // 16) & (lane // 64 == zh)
    chosen = chosen & (rr // 128 * 4 + lax.rem(lane, 64) // 16 == lax.rem(cc, 16))
    pick[...] = jnp.where(chosen, jnp.float32(1), jnp.float32(0))

    total = lp[y, x]
    for j in range(1, 16):
        fn(j).wait_recv()
    for j in range(1, 16):
        total += lr[j]
    fo[...] = total

    def fg(j):
        far_z, gg = j // 4, lax.rem(g + j, 4)
        zz = zh + far_z - 2 * zh * far_z
        return send(fo, fr.at[far_z, g], fg_s.at[j], fg_r.at[j], (gg, y * 8 + zz * 4 + x))

    for j in (6, 5, 7, 2, 4, 3, 1):
        fg(j).start()
    fr[0, g] = total
    for j in range(1, 8):
        fg(j).wait_recv()
    sums = jnp.concatenate([fr[0, p] + fr[1, p] for p in range(4)], axis=1)
    res = jnp.dot(sums, pick[...], precision=lax.Precision.HIGHEST, preferred_element_type=F32)
    for a in range(4):
        out_ref[:, a, :] = res[:, 16 * a : 16 * a + 16]

    @pl.loop(1, 16)
    def _(j):
        fn(j).wait_send()

    for j in range(1, 8):
        fg(j).wait_send()


def local(row_orbitals, orbitals, fitting, partner_vertex, amplitudes):
    ng, na = fitting.shape
    dma = pltpu.SemaphoreType.DMA
    return pl.pallas_call(
        kernel,
        out_shape=jax.ShapeDtypeStruct((8, 4, 16), F32),
        in_specs=[pl.BlockSpec(memory_space=pl.ANY)] * 5,
        out_specs=pl.BlockSpec(memory_space=pltpu.VMEM),
        scratch_shapes=[
            pltpu.VMEM((4, ng), BF),
            pltpu.VMEM((4, 16, ng), BF),
            pltpu.VMEM((512, ng), BF),
            pltpu.VMEM((ng, na), BF),
            pltpu.VMEM((256, ng), BF),
            pltpu.VMEM((8, 2, 4, 32, na), BF),
            pltpu.VMEM((8, 2, 2, 16, na), BF),
            pltpu.VMEM((8, 2, 2, 16, na), BF),
            pltpu.VMEM((8, 2, 2, 16, na), BF),
            pltpu.VMEM((8, 2, 2, 16, na), BF),
            pltpu.VMEM((2, 2, 4, 32, na), BF),
            pltpu.VMEM((2, 2, 2, 16, na), BF),
            pltpu.VMEM((2, 2, 2, 16, na), BF),
            pltpu.VMEM((2, 2, 2, 16, na), BF),
            pltpu.VMEM((2, 2, 2, 16, na), BF),
            pltpu.VMEM((2, 32, na), BF),
            pltpu.VMEM((2, 32, na), BF),
            pltpu.VMEM((2, 4, 64, na), BF),
            pltpu.VMEM((256, na), BF),
            pltpu.VMEM((4, 4, 4, 16, na), BF),
            pltpu.VMEM((256, 16, 512), BF),
            pltpu.VMEM((64, 16, 256), BF),
            pltpu.VMEM((256, 16, 256), BF),
            pltpu.VMEM((2, 16, 256, 256), BF),
            pltpu.VMEM((16, 64, 256), BF),
            pltpu.VMEM((256, 64), F32),
            pltpu.VMEM((4, 4, 8, 128), F32),
            pltpu.VMEM((16, 8, 128), F32),
            pltpu.VMEM((8, 128), F32),
            pltpu.VMEM((2, 4, 8, 128), F32),
            pltpu.VMEM((512, 64), F32),
            pltpu.VMEM((256, 256), BF),
            dma((18,)),
            dma((40,)), dma((40,)),
            dma((8, 2, 6)), dma((8, 2, 6)),
            dma((2, 2, 6)), dma((2, 2, 6)),
            dma((2,)), dma((2,)),
            dma((14,)), dma((14,)),
            dma((4,)), dma((4,)),
            dma((16,)), dma((16,)),
            dma((8,)), dma((8,)),
        ],
        compiler_params=pltpu.CompilerParams(
            collective_id=0, has_side_effects=True, vmem_limit_bytes=60 * 1024 * 1024
        ),
    )(row_orbitals, orbitals, fitting, partner_vertex, amplitudes)


def solution(mesh):
    in_specs = (P("grp", "pw"), P(None, "pw"), P("pw", None), P("grp", "pw", None), P(None, "pw", None))
    return jax.shard_map(
        local, mesh=mesh, in_specs=in_specs, out_specs=P("pw", "grp", None), check_vma=False
    )
```

```python
import jax
import jax.numpy as jnp
from jax import lax
from jax.experimental import pallas as pl
from jax.experimental.pallas import tpu as pltpu
from jax.sharding import PartitionSpec as P

MESH = pl.DeviceIdType.MESH
BF = jnp.bfloat16
F32 = jnp.float32
NT = 256
FAR_FIRST = (10, 6, 14, 9, 11, 2, 8, 5, 7, 13, 15, 1, 3, 4, 12)


def kernel(
    rows_h, orb_h, fit_h, pv_h, amp_h, out_ref,
    rows_v, rowsb, orb, fit, pair, part, r1, r2, r3, t3, s1, u1, u2, u3, v3, s2b, zr,
    vall, vperm, pvall, amp, ah, ampb, ampt, rg, lacc, lp, lr, fo, fr, pick, perm,
    ld, ag_s, ag_r, rs_s, rs_r, st_s, st_r, z_s, z_r, ve_s, ve_r, am_s, am_r, fn_s, fn_r, fg_s, fg_r,
):
    g = lax.axis_index("grp")
    w = lax.axis_index("pw")
    y, zh, x = w // 8, lax.rem(w // 4, 2), lax.rem(w, 4)
    ng = rows_v.shape[1]
    na = fit.shape[1]
    core = lax.rem(g, 2)
    g_core, g_chip = g + 1 - 2 * core, lax.rem(g + 2, 4)
    w_far = w + 4 - 8 * zh

    def dev(yy, zz, xx):
        return (g, yy * 8 + zz * 4 + xx)

    def up(v, by=1):
        return lax.rem(v + by, 4)

    def send(src, dst, ss, rs, to):
        return pltpu.make_async_remote_copy(
            src_ref=src, dst_ref=dst, send_sem=ss, recv_sem=rs, device_id=to, device_id_type=MESH
        )

    def piece(d, h):
        rows = pl.ds(pl.multiple_of(128 * d + 64 * (h * zh + (1 - h) * (1 - zh)), 64), 64)
        return pltpu.make_async_copy(orb_h.at[rows, :], orb.at[rows, :], ld.at[7 + 4 * h + d])

    def fit_tile(t):
        rows = slice(t * (ng // 4), (t + 1) * (ng // 4))
        return pltpu.make_async_copy(fit_h.at[rows], fit.at[rows], ld.at[3 + t])

    tiles = na // NT
    l_rows = pltpu.make_async_copy(rows_h, rows_v, ld.at[0])

    def l_amp(k):
        rows = pl.ds(pl.multiple_of(64 * lax.rem(g + 2 + k, 4), 64), 64)
        return pltpu.make_async_copy(amp_h.at[rows], amp.at[rows], ld.at[14 + k if k else 1])

    l_pv = pltpu.make_async_copy(pv_h, pvall.at[:, y, x], ld.at[2])
    for c in (l_rows, l_amp(0), *(piece(d, 0) for d in range(4)), *(fit_tile(t) for t in range(4)), l_pv):
        c.start()

    barrier = pltpu.get_barrier_semaphore()

    for j in FAR_FIRST:
        peer = dev(up(y, j // 4), zh, up(x, j % 4))
        pl.semaphore_signal(barrier, inc=1, device_id=peer, device_id_type=MESH)

    @pl.loop(1, 8)
    def _(j):
        peer = (lax.rem(g + j, 4), w + (j // 4) * (4 - 8 * zh))
        pl.semaphore_signal(barrier, inc=1, device_id=peer, device_id_type=MESH)

    ring = {0: (dev(y, zh, up(x)), dev(y, zh, up(x, 3))), 1: (dev(up(y), zh, x), dev(up(y, 3), zh, x))}
    ag1, ag1f, ag2, ag2f = {}, {}, {}, {}
    n = 0

    def ag(into, key, src, ref, to):
        nonlocal n
        into[key] = send(src, ref, ag_s.at[n], ag_r.at[n], to)
        n += 1

    for f in (0, 1):
        for side in (0, 1):
            to, back, b = ring[f][side], 3 - 2 * side, 2 * f + side
            pair_of = slice(2 * f, 2 * f + 2)
            own = pv_h.at[pair_of]
            ag(ag1, (f, side), own, pvall.at[pair_of, y, x], to)
            ref = pvall.at[b, y, up(x, back)] if f == 0 else pvall.at[b, up(y, back), x]
            ag(ag1f, (f, side), ref, ref, to)
            to = ring[1 - f][side]
            for d in range(4):
                ref = pvall.at[pair_of, y, up(x, d)] if f == 0 else pvall.at[pair_of, up(y, d), x]
                ag(ag2, (f, side, d), own if d == 0 else ref, ref, to)
            for d in range(4):
                ref = pvall.at[b, up(y, back), up(x, d)] if f == 0 else pvall.at[b, up(y, d), up(x, back)]
                ag(ag2f, (f, side, d), ref, ref, to)

    def each(msgs, act, *p):
        for f in (0, 1):
            for side in (0, 1):
                getattr(msgs[(f, side, *p)], act)()

    def quarter(q):
        return pl.ds(pl.multiple_of(64 * q, 64), 64)

    mine, theirs = g, lax.rem(g + 2, 4)

    def am(k):
        src, rows, to = (
            (ah, theirs, (g_chip, w_far)),
            (ampb.at[quarter(mine)], mine, (g_chip, w)),
            (ampb.at[quarter(mine)], mine, (g_core, w)),
            (ampb.at[quarter(theirs)], theirs, (g_core, w)),
        )[k]
        return send(src, ampb.at[quarter(rows)], am_s.at[k], am_r.at[k], to)

    place = (x, y)

    def rs(s, e, m):
        q, (right, left) = place[e], ring[e]
        src, dst, to = {
            0: lambda: (part.at[s, e, up(q, 2), 0:16], r1.at[s, e, 0], right),
            1: lambda: (part.at[s, e, up(q, 2), 16:32], r1.at[s, e, 1], left),
            2: lambda: (part.at[s, e, up(q, 1), 16:32], r2.at[s, e, 0], right),
            3: lambda: (part.at[s, e, up(q, 3), 0:16], r2.at[s, e, 1], left),
            4: lambda: (t3.at[s, e, 0], r3.at[s, e, 0], right),
            5: lambda: (t3.at[s, e, 1], r3.at[s, e, 1], left),
        }[m]()
        return send(src, dst, rs_s.at[s, e, m], rs_r.at[s, e, m], to)

    def st(h, e, m):
        right, left = ring[1 - e]
        src, dst, to = {
            0: lambda: (s1.at[h, e, 0, 0:16], u1.at[h, e, 0], right),
            1: lambda: (s1.at[h, e, 0, 16:32], u1.at[h, e, 1], left),
            2: lambda: (s1.at[h, e, 1, 16:32], u2.at[h, e, 0], right),
            3: lambda: (s1.at[h, e, 2, 0:16], u2.at[h, e, 1], left),
            4: lambda: (v3.at[h, e, 0], u3.at[h, e, 0], right),
            5: lambda: (v3.at[h, e, 1], u3.at[h, e, 1], left),
        }[m]()
        return send(src, dst, st_s.at[h, e, m], st_r.at[h, e, m], to)

    def sends(s, ms):
        for m in ms:
            for e in (0, 1):
                rs(s, e, m).start()

    def middle(s):
        for e in (0, 1):
            for side in (0, 1):
                half = slice(16 * side, 16 * side + 16)
                rs(s, e, side).wait_recv()
                mine = part[s, e, up(place[e], 1 + 2 * side), half].astype(F32)
                t3[s, e, side] = (mine + r1[s, e, side].astype(F32)).astype(BF)
                rs(s, e, 4 + side).start()

    def first_sum(s, e):
        for m in (2, 3, 4, 5):
            rs(s, e, m).wait_recv()
        q = place[e]
        lo = part[s, e, q, 0:16].astype(F32) + r3[s, e, 0].astype(F32) + r2[s, e, 1].astype(F32)
        hi = part[s, e, q, 16:32].astype(F32) + r2[s, e, 0].astype(F32) + r3[s, e, 1].astype(F32)
        return lo, hi

    def finish(s, h, k):
        for e in (0, 1):
            lo, hi = first_sum(s, e)
            s1[h, e, k, 0:16] = lo.astype(BF)
            s1[h, e, k, 16:32] = hi.astype(BF)
            for m in ((0, 1), (2,), (3,))[k]:
                st(h, e, m).start()

    def third(h, side):
        half = slice(16 * side, 16 * side + 16)
        for e in (0, 1):
            st(h, e, side).wait_recv()
            v3[h, e, side] = (s1[h, e, 1 + side, half].astype(F32) + u1[h, e, side].astype(F32)).astype(BF)
            st(h, e, 4 + side).start()

    def last_sum(h, e):
        lo, hi = first_sum(4 * h + 3, e)
        for m in (2, 3, 4, 5):
            st(h, e, m).wait_recv()
        lo = lo + u3[h, e, 0].astype(F32) + u2[h, e, 1].astype(F32)
        hi = hi + u2[h, e, 0].astype(F32) + u3[h, e, 1].astype(F32)
        return lo, hi

    zsend = [
        send(s2b.at[e], zr.at[e], z_s.at[e], z_r.at[e], dev(y, 1 - zh, x)) for e in (0, 1)
    ]

    def gen(s):
        h, k = s // 4, lax.rem(s, 4)
        off = jnp.where(k == 0, 2, jnp.where(k == 1, 1, jnp.where(k == 2, 3, 0)))
        z64 = 64 * (h * zh + (1 - h) * (1 - zh))
        for e in (0, 1):
            for j in range(4):
                c0 = 128 * up(y, off) + 16 * j if e == 0 else 128 * j + 16 * up(x, off)
                ob = orb[pl.ds(pl.multiple_of(c0 + z64, 16), 16), :]
                for a in (0, 1):
                    row = 128 * e + 32 * j + 16 * a
                    pair[row : row + 16, :] = rowsb[2 * e + a] * ob

    def mm(s, t):
        acc = jnp.dot(pair[...], fit[:, t * NT : (t + 1) * NT], preferred_element_type=F32)
        part[s, :, :, :, t * NT : (t + 1) * NT] = acc.astype(BF).reshape(2, 4, 32, NT)

    pl.semaphore_wait(barrier, 22)
    each(ag1, "start")
    each(ag2, "start", 0)
    ii = lax.broadcasted_iota(jnp.int32, (256, 256), 0)
    jj = lax.broadcasted_iota(jnp.int32, (256, 256), 1)
    perm[...] = jnp.where(
        jj == lax.rem(ii, 16) * 16 + ii // 16, jnp.float32(1), jnp.float32(0)
    ).astype(BF)
    l_rows.wait()
    for a in range(4):
        rowsb[a] = jnp.broadcast_to(rows_v[a : a + 1, :], (16, ng))
    low = lax.broadcasted_iota(jnp.int32, (1, 1, 128), 2) < 64

    def lanes_of(rows, plane):
        first, parts = plane == 0, []
        for m in (0, 1):
            lo = amp[rows, :, 256 * m : 256 * m + 128]
            hi = amp[rows, :, 256 * m + 128 : 256 * m + 256]
            lo = jnp.where(first, lo, pltpu.roll(lo, 64, 2))
            hi = jnp.where(first, pltpu.roll(hi, 64, 2), hi)
            parts.append(jnp.where(low, lo, hi))
        return jnp.concatenate(parts, axis=2)

    l_amp(0).wait()
    @pl.loop(0, 4)
    def _(i):
        rows = pl.ds(pl.multiple_of(64 * theirs + i * 16, 16), 16)
        ah[pl.ds(pl.multiple_of(i * 16, 16), 16)] = lanes_of(rows, 1 - zh)

    am(0).start()
    for d in range(4):
        piece(d, 1).start()
    for k in (1, 2, 3):
        l_amp(k).start()
    for d in range(4):
        piece(d, 0).wait()
    for t in range(4):
        fit_tile(t).wait()

    @pl.loop(0, 8)
    def _(s):
        gen(s)
        for t in range(tiles):
            mm(s, t)
        sends(s, (0, 1))

        @pl.when(s >= 2)
        def _():
            middle(s - 2)

        @pl.when(s < 7)
        def _():
            sends(s, (2, 3))

        @pl.when(s == 0)
        def _():
            each(ag1, "wait_recv")
            each(ag1f, "start")
            each(ag2, "start", 1)
            for d in range(4):
                piece(d, 1).wait()

        @pl.when(s == 4)
        def _():
            am(0).wait_recv()
            am(1).start()
            am(2).start()

        @pl.when(s == 4)
        def _():
            finish(0, 0, 0)

        @pl.when(s == 5)
        def _():
            finish(1, 0, 1)

        @pl.when(s == 6)
        def _():
            third(0, 0)
            finish(2, 0, 2)
            third(0, 1)


    def turn(block, dst, lo, hi):
        @pl.loop(lo, hi, step=2)
        def _(i):
            for k in (0, 1):
                rows = pl.ds(pl.multiple_of((i + k) * 16, 16), 16)
                turned = jnp.dot(perm[...], block(rows).reshape(256, 256), preferred_element_type=F32)
                dst[:, rows, :] = turned.astype(BF).reshape(16, 16, 256)

    def own_lanes(rows):
        return lanes_of(rows, zh)

    finish(4, 1, 0)
    middle(6)
    sends(jnp.int32(7), (2, 3))
    for k in (1, 2, 3):
        l_amp(k).wait()
    turn(own_lanes, ampt.at[0], 0, 8)
    turn(own_lanes, ampt.at[0], 8, 16)
    for e in (0, 1):
        lo, hi = last_sum(0, e)
        s2b[e, 0:16] = lo.astype(BF)
        s2b[e, 16:32] = hi.astype(BF)
        zsend[e].start()
    middle(7)
    finish(5, 1, 1)
    third(1, 0)
    am(1).wait_recv()
    am(3).start()
    finish(6, 1, 2)
    third(1, 1)
    each(ag1f, "wait_recv")
    for d in (3, 2):
        each(ag2, "start", d)
    for d in (0, 1):
        each(ag2, "wait_recv", d)
        each(ag2f, "start", d)

    def turn_far():
        am(2).wait_recv()
        am(3).wait_recv()
        turn(lambda rows: ampb[rows], ampt.at[1], 0, 16)

    pl.when(core == 0)(turn_far)
    mate, cross, twin = (g_chip, w), (g_chip, w_far), (g_core, w)
    ve = []

    def share(ref, to):
        ve.append(send(ref, ref, ve_s.at[len(ve)], ve_r.at[len(ve)], to))
        return ve[-1]

    to_mate, to_cross, to_twin = [], [], []
    halves = (slice(0, 32), slice(32, 64))
    for e, v in enumerate(halves):
        lo, hi = last_sum(1, e)
        zsend[e].wait_recv()
        vall[zh, g, 32 * e : 32 * e + 16] = (lo + zr[e, 0:16].astype(F32)).astype(BF)
        vall[zh, g, 32 * e + 16 : 32 * e + 32] = (hi + zr[e, 16:32].astype(F32)).astype(BF)
        own = vall.at[zh, g, v]
        for sent, to in ((to_mate, mate), (to_cross, cross), (to_twin, twin)):
            sent.append(share(own, to))
            sent[-1].start()
    of_mate = [vall.at[zh, g_chip, v] for v in halves]
    of_cross = [vall.at[1 - zh, g_chip, v] for v in halves]
    of_far = [vall.at[1 - zh, g, v] for v in halves]
    far = [share(of_cross[0], mate), share(of_mate[1], cross)]
    twin_mate = [share(r, twin) for r in of_mate]
    twin_cross = [share(r, twin) for r in of_cross]
    twin_far = [share(r, twin) for r in of_far]

    pl.when(core == 1)(turn_far)
    for d in (3, 2):
        each(ag2, "wait_recv", d)
        each(ag2f, "start", d)
    to_mate[0].wait_recv()
    twin_mate[0].start()
    to_cross[0].wait_recv()
    far[0].start()
    twin_cross[0].start()
    to_mate[1].wait_recv()
    far[1].start()
    twin_mate[1].start()
    to_cross[1].wait_recv()
    twin_cross[1].start()
    for c in (*to_twin, *twin_mate):
        c.wait_recv()

    nt = (((1,), (1,)), ((), ()))

    def rungs(z):
        vperm[...] = jnp.dot(perm[...], vall[z].reshape(256, na), preferred_element_type=F32).astype(BF)
        for b in range(4):
            rung = lax.dot_general(vperm[...], pvall[b].reshape(256, na), nt, preferred_element_type=F32)
            rg[:, b * 16 : b * 16 + 16, :] = rung.astype(BF).reshape(16, 16, 256)

    def ladder(k):
        acc = jnp.zeros((256, 64), F32)
        for c in range(16):
            acc += lax.dot_general(ampt[k, c], rg[c], nt, preferred_element_type=F32)
        return acc

    l_pv.wait()
    for d in range(4):
        each(ag2f, "wait_recv", d)
    rungs(zh)
    for k in (0, 1):
        far[k].wait_recv()
        twin_far[k].start()
    lacc[...] = ladder(0)
    for c in (*twin_cross, *twin_far):
        c.wait_recv()
    rungs(1 - zh)
    both = (lacc[...] + ladder(1)).reshape(4, 2, 4, 8, 64)
    lp[..., 0:64] = both[:, 0]
    lp[..., 64:128] = both[:, 1]

    def fn(j):
        yy, xx = up(y, j // 4), up(x, lax.rem(j, 4))
        return send(lp.at[yy, xx], lr.at[j], fn_s.at[j], fn_r.at[j], dev(yy, zh, xx))

    for j in FAR_FIRST:
        fn(j).start()

    for msgs in (ag1, ag1f, ag2, ag2f):
        for c in msgs.values():
            c.wait_send()
    for e in (0, 1):
        for m in range(6):
            for h in (0, 1):
                st(h, e, m).wait_send()

    @pl.loop(0, 8)
    def _(s):
        for e in (0, 1):
            for m in range(6):
                rs(s, e, m).wait_send()

    for k in range(4):
        am(k).wait_send()
    for c in (*zsend, *ve):
        c.wait_send()

    rr = lax.broadcasted_iota(jnp.int32, (512, 64), 0)
    cc = lax.broadcasted_iota(jnp.int32, (512, 64), 1)
    lane = lax.rem(rr, 128)
    chosen = (lax.rem(lane, 16) == g * 4 + cc // 16) & (lane // 64 == zh)
    chosen = chosen & (rr // 128 * 4 + lax.rem(lane, 64) // 16 == lax.rem(cc, 16))
    pick[...] = jnp.where(chosen, jnp.float32(1), jnp.float32(0))

    total = lp[y, x]
    for j in range(1, 16):
        fn(j).wait_recv()
    for j in range(1, 16):
        total += lr[j]
    fo[...] = total

    def fg(j):
        far_z, gg = j // 4, lax.rem(g + j, 4)
        zz = zh + far_z - 2 * zh * far_z
        return send(fo, fr.at[far_z, g], fg_s.at[j], fg_r.at[j], (gg, y * 8 + zz * 4 + x))

    for j in (6, 5, 7, 2, 4, 3, 1):
        fg(j).start()
    fr[0, g] = total
    for j in range(1, 8):
        fg(j).wait_recv()
    sums = jnp.concatenate([fr[0, p] + fr[1, p] for p in range(4)], axis=1)
    res = jnp.dot(sums, pick[...], precision=lax.Precision.HIGHEST, preferred_element_type=F32)
    for a in range(4):
        out_ref[:, a, :] = res[:, 16 * a : 16 * a + 16]

    @pl.loop(1, 16)
    def _(j):
        fn(j).wait_send()

    for j in range(1, 8):
        fg(j).wait_send()


def local(row_orbitals, orbitals, fitting, partner_vertex, amplitudes):
    ng, na = fitting.shape
    dma = pltpu.SemaphoreType.DMA
    return pl.pallas_call(
        kernel,
        out_shape=jax.ShapeDtypeStruct((8, 4, 16), F32),
        in_specs=[pl.BlockSpec(memory_space=pl.ANY)] * 5,
        out_specs=pl.BlockSpec(memory_space=pltpu.VMEM),
        scratch_shapes=[
            pltpu.VMEM((4, ng), BF),
            pltpu.VMEM((4, 16, ng), BF),
            pltpu.VMEM((512, ng), BF),
            pltpu.VMEM((ng, na), BF),
            pltpu.VMEM((256, ng), BF),
            pltpu.VMEM((8, 2, 4, 32, na), BF),
            pltpu.VMEM((8, 2, 2, 16, na), BF),
            pltpu.VMEM((8, 2, 2, 16, na), BF),
            pltpu.VMEM((8, 2, 2, 16, na), BF),
            pltpu.VMEM((8, 2, 2, 16, na), BF),
            pltpu.VMEM((2, 2, 4, 32, na), BF),
            pltpu.VMEM((2, 2, 2, 16, na), BF),
            pltpu.VMEM((2, 2, 2, 16, na), BF),
            pltpu.VMEM((2, 2, 2, 16, na), BF),
            pltpu.VMEM((2, 2, 2, 16, na), BF),
            pltpu.VMEM((2, 32, na), BF),
            pltpu.VMEM((2, 32, na), BF),
            pltpu.VMEM((2, 4, 64, na), BF),
            pltpu.VMEM((256, na), BF),
            pltpu.VMEM((4, 4, 4, 16, na), BF),
            pltpu.VMEM((256, 16, 512), BF),
            pltpu.VMEM((64, 16, 256), BF),
            pltpu.VMEM((256, 16, 256), BF),
            pltpu.VMEM((2, 16, 256, 256), BF),
            pltpu.VMEM((16, 64, 256), BF),
            pltpu.VMEM((256, 64), F32),
            pltpu.VMEM((4, 4, 8, 128), F32),
            pltpu.VMEM((16, 8, 128), F32),
            pltpu.VMEM((8, 128), F32),
            pltpu.VMEM((2, 4, 8, 128), F32),
            pltpu.VMEM((512, 64), F32),
            pltpu.VMEM((256, 256), BF),
            dma((18,)),
            dma((40,)), dma((40,)),
            dma((8, 2, 6)), dma((8, 2, 6)),
            dma((2, 2, 6)), dma((2, 2, 6)),
            dma((2,)), dma((2,)),
            dma((14,)), dma((14,)),
            dma((4,)), dma((4,)),
            dma((16,)), dma((16,)),
            dma((8,)), dma((8,)),
        ],
        compiler_params=pltpu.CompilerParams(
            collective_id=0, has_side_effects=True, vmem_limit_bytes=60 * 1024 * 1024
        ),
    )(row_orbitals, orbitals, fitting, partner_vertex, amplitudes)


def solution(mesh):
    in_specs = (P("grp", "pw"), P(None, "pw"), P("pw", None), P("grp", "pw", None), P(None, "pw", None))
    return jax.shard_map(
        local, mesh=mesh, in_specs=in_specs, out_specs=P("pw", "grp", None), check_vma=False
    )
```
